256 devices in a mesh: grp: 4 (over y_lo, core), tm: 64 (over z, y_hi, x).
Axes of the slice: x: 4, y: 4 (y_hi: 2, y_lo: 2; y = y_hi * 2 + y_lo), z: 8, core: 2. Of those that a mesh axis runs over, the one named last changes fastest.
Arguments:
- records: bfloat16 [24576, 512], P('tm', 'grp'), may hold values from -6 to 6
- measured: bfloat16 [24576, 512], P('tm', 'grp'), may hold values from -6 to 6
- markov_params: float32 [64, 512, 512], P('tm', 'grp'), may hold values from -6 to 6
- seg_lengths: int32 [64], P('tm'), may hold values from 1 to 384, 15360 in all
Outputs:
- new_params: float32 [64, 512, 512], P('tm', 'grp')
- residual: bfloat16 [24576, 512], P('tm', 'grp')
The draws below stay inside these ranges and needn't reach their ends.
Inputs may be any that keep to these rules, and one draw needn't show every extreme that they name: seg_lengths of all 64 segments sum to 15360; some segment is full.
All inputs are finite; a program needn't handle non-finite values. No bound on the sum of `seg_lengths` on one device may be relied on, other than what follows from the above.
Results may differ from the reference program's by a relative error of at most 0.0039.
Values may be sent and summed in bfloat16 or wider, within the bound.
A program may use at most 64 MiB of HBM per device.

```python
import math
import jax
import jax.numpy as jnp
import numpy as np
from jax import lax

P_SIZE = 512
M = 512
LAGS = 64
TIME_DEV = 384
TIME = 24576
SEGS = 64


def steps_of(own_key, dims, split, smallest, top_value):
    gain, own = 1.0, jax.random.fold_in(own_key, 6)
    for dim, blocks in split:
        steps = jnp.exp(jax.random.uniform(jax.random.fold_in(own, dim), (blocks,), jnp.float32, smallest / len(split), top_value / len(split)))
        gain = gain * jnp.repeat(steps, dims[dim] // blocks).reshape([-1 if axis == dim else 1 for axis in range(len(dims))])
    return gain


def split_up(number_of, total, reach, skew):
    portions = [(1 << 20) // math.isqrt(rank ** skew) + 1 for rank in range(2, number_of + 1)]
    rest, counts = total - reach - (number_of - 1), [1] * (number_of - 1)
    while rest > 0:
        movable = [i for i in range(number_of - 1) if counts[i] < reach]
        mass, left = sum([portions[i] for i in movable]), rest
        for i in movable:
            more = min(reach - counts[i], max(1, left * portions[i] // mass), rest)
            counts[i] = counts[i] + more
            rest = rest - more
    return np.array([reach] + counts)


def ragged_sizes(key, number_of, total, bound, lean):
    if number_of == 2:
        one = jax.random.randint(key, (), max(1, total - bound), min(bound, total - 1) + 1)
        return jnp.stack([one, total - one])
    sizes = jnp.asarray(split_up(number_of, total, bound, lean), jnp.int32)
    twos = (number_of - 1) // 2
    source_of, sink = sizes[1:1 + 2 * twos:2], sizes[2:2 + 2 * twos:2]
    slack = jnp.minimum(source_of - 1, bound - sink)
    passed = jax.random.randint(jax.random.fold_in(key, 1), (twos,), 0, 1 << 20) % (slack + 1)
    sizes = sizes.at[1:1 + 2 * twos:2].set(source_of - passed).at[2:2 + 2 * twos:2].set(sink + passed)
    return sizes[jax.random.permutation(jax.random.fold_in(key, 2), number_of)]


def scatter_about(stream_key, shape, deviation, most, cuts=(), kind=jnp.bfloat16):
    drawn = jax.random.normal(stream_key, shape, jnp.float32) * deviation
    if len(cuts) > 0:
        drawn = steps_of(stream_key, shape, cuts, -0.22, 0.18) * drawn
    return jnp.clip(drawn, min=-most, max=most).astype(kind)


def setup_inputs(seed: int = 0) -> dict:
    splits = jax.random.split(jax.random.key(seed), 5)
    return {
        "records": scatter_about(splits[0], (TIME, M), 1.0, 6.0, ((0, 64), (1, 4))),
        "measured": scatter_about(splits[1], (TIME, P_SIZE), 1.0, 6.0, ((0, 64), (1, 4))),
        "markov_params": scatter_about(splits[2], (LAGS, P_SIZE, M), 1.0, 6.0, ((0, 64), (1, 4)), jnp.float32),
        "seg_lengths": ragged_sizes(splits[3], SEGS, SEGS * TIME_DEV * 5 // 8, TIME_DEV, 2).astype(jnp.int32),
    }


def reference(records, measured, markov_params, seg_lengths):
    lag_span = LAGS - 1
    padded = jnp.concatenate([jnp.zeros((lag_span, M), records.dtype), records], axis=0)
    weights = markov_params.astype(jnp.bfloat16)
    lag_list = jnp.arange(LAGS, dtype=jnp.int32)

    def add_lag(running, lag_item):
        lag_weight, lag_index = lag_item
        window = lax.dynamic_slice_in_dim(padded, (lag_span - lag_index).astype(jnp.int32), TIME, 0)
        return (running + jnp.dot(window, lag_weight.T, preferred_element_type=jnp.float32), None)
    summed, unused = lax.scan(add_lag, jnp.zeros((TIME, P_SIZE), jnp.float32), (weights, lag_list))
    predicted = summed * (1.0 / math.sqrt(LAGS * M))
    position = jnp.arange(TIME, dtype=jnp.int32)
    live_mask = position % TIME_DEV < seg_lengths[position // TIME_DEV]
    residual = jnp.where(live_mask[:, None], measured.astype(jnp.float32) - predicted, 0.0).astype(jnp.bfloat16)
    dir_scale = 1.0 / math.sqrt(TIME)

    def lag_term(lag_index):
        window = lax.dynamic_slice_in_dim(padded, (lag_span - lag_index).astype(jnp.int32), TIME, 0)
        return jnp.dot(residual.T, window, preferred_element_type=jnp.float32) * dir_scale
    direction = lax.map(lag_term, lag_list)
    new_params = markov_params + 0.5 * direction
    return (new_params, residual)
```

```python
import math

import jax
import jax.numpy as jnp
from jax import lax
from jax.experimental import pallas as pl
from jax.experimental.pallas import tpu as pltpu
from jax.sharding import PartitionSpec as P

M = 512
LAGS = 64
BF = jnp.bfloat16
F32 = jnp.float32


def body(len_ref, rec_ref, meas_ref, par_ref, new_ref, res_ref, wsend, wbuf, xraw, xf, xpf, xs, lsend, lraw, mraw, mf,
         acc, csend, crecv, rall, rt, rout, rres, dall, dxs, dxr, gs, gr, fs, fr,
         sb1, rb1, sa, ra, sm, rm, sh, rh, sring, rring, spair, rpair, sc, rc, sr, rr, sdx, rdx, sg, rg, sf, rf):
    tm = lax.axis_index("tm")
    grp = lax.axis_index("grp")
    z = tm // 8
    yh = (tm // 4) % 2
    x = tm % 4
    yl = grp // 2
    core = grp % 2
    q = yl * 2 + yh

    def spread(j):
        return z * 8 + core * 4 + j, yl * 2 + yh

    def t_out(c):
        return z * 8 + (c % 2) * 4 + grp, (c // 2) * 2 + yh

    def t_in(j):
        return z * 8 + core * 4 + j, x

    def peer(j):
        return z * 8 + (j % 2) * 4 + x, (j // 2) * 2 + core

    def along(step):
        return lax.rem(z + step + 8, 8) * 8 + yh * 4 + x, grp

    partner = (tm, yl * 2 + 1 - core)
    ahead = (lax.rem(z + core, 8) * 8 + yh * 4 + x, yl * 2 + 1 - core)
    behind = (lax.rem(z + core + 7, 8) * 8 + yh * 4 + x, yl * 2 + 1 - core)

    def is_me(dev):
        return jnp.logical_and(dev[0] == tm, dev[1] == grp)

    def send(src, dst, ssem, rsem, dev):
        return pltpu.make_async_remote_copy(src_ref=src, dst_ref=dst, send_sem=ssem, recv_sem=rsem,
                                            device_id={"tm": dev[0], "grp": dev[1]},
                                            device_id_type=pl.DeviceIdType.MESH)

    def start_any(src, dst, ssem, rsem, dev):
        me = is_me(dev)

        @pl.when(me)
        def _():
            pltpu.make_async_copy(src, dst, rsem).start()

        @pl.when(jnp.logical_not(me))
        def _():
            send(src, dst, ssem, rsem, dev).start()

    def done_any(src, dst, ssem, rsem, dev):
        @pl.when(jnp.logical_not(is_me(dev)))
        def _():
            send(src, dst, ssem, rsem, dev).wait_send()

    def got(dst, ssem, rsem):
        send(dst, dst, ssem, rsem, partner).wait_recv()

    barrier = pltpu.get_barrier_semaphore()
    count = jnp.int32(0)
    friends = [spread(j) for j in range(4)] + [t_out(j) for j in range(4)] + [t_in(j) for j in range(4)]
    for dev in friends:
        other = jnp.logical_not(is_me(dev))
        count = count + other.astype(jnp.int32)

        @pl.when(other)
        def _():
            pl.semaphore_signal(barrier, inc=1, device_id={"tm": dev[0], "grp": dev[1]},
                                device_id_type=pl.DeviceIdType.MESH)
    sure = [peer(lax.rem(q + k, 4)) for k in (1, 2, 3)] + [along(1), along(-1), partner, ahead, behind]
    for dev in sure:
        pl.semaphore_signal(barrier, inc=1, device_id={"tm": dev[0], "grp": dev[1]},
                            device_id_type=pl.DeviceIdType.MESH)
    for c in range(4):
        wsend[c] = par_ref[:, c * 128:(c + 1) * 128].astype(BF)
    lsend[...] = jnp.full((8, 128), len_ref[0], jnp.int32).astype(F32)
    pl.semaphore_wait(barrier, count + len(sure))

    for c in range(4):
        start_any(wsend.at[c], wbuf.at[tm], sb1.at[c], rb1.at[x], t_out(c))
    own_rows = pl.ds(pl.multiple_of(64 + 384 * x, 64), 384)
    for j in range(4):
        start_any(rec_ref, xraw.at[own_rows], sa.at[j], ra.at[x], spread(j))
    start_any(meas_ref, mraw, sm.at[0], rm.at[0], t_out(x))
    start_any(lsend, lraw, sm.at[1], rm.at[1], t_out(x))

    def pair_lags(chunk, half, sub):
        return wbuf.at[pl.ds(lax.rem(chunk + 8, 8) * 8 + half * 4 + sub * 2, 2)]

    def ring_send(way, step, sub):
        chunk = z - step if way == 0 else z + step
        ref = pair_lags(chunk, core, sub)
        return send(ref, ref, sring.at[way, step, sub], rring.at[way, step, sub], along(1 if way == 0 else -1))

    def pair_send(chunk_slot, chunk, sub):
        ref = pair_lags(chunk, core, sub)
        return send(ref, ref, spair.at[chunk_slot, sub], rpair.at[chunk_slot, sub], partner)

    def ring_got(way, step, sub):
        chunk = z - step if way == 0 else z + step
        got(pair_lags(chunk, core, sub), sring.at[way, step - 1, sub], rring.at[way, step - 1, sub])

    def pair_got(chunk_slot, chunk, sub):
        got(pair_lags(chunk, 1 - core, sub), spair.at[chunk_slot, sub], rpair.at[chunk_slot, sub])

    sent = []

    def go(desc):
        desc.start()
        sent.append(desc)

    for sub in range(2):
        for j in (2 * sub, 2 * sub + 1):
            got(wbuf.at[z * 8 + core * 4 + j], sb1.at[j], rb1.at[j])
        go(ring_send(0, 0, sub))
        go(ring_send(1, 0, sub))
        go(pair_send(0, z, sub))

    got(xraw.at[pl.ds(64 + 384 * 3, 384)], sa.at[3], ra.at[3])
    go(send(xraw.at[pl.ds(64 + 1536 - 64, 64)], xraw.at[pl.ds(0, 64)], sh.at[0], rh.at[0], ahead))
    for j in range(3):
        got(xraw.at[pl.ds(64 + 384 * j, 384)], sa.at[j], ra.at[j])
    got(xraw.at[pl.ds(0, 64)], sh.at[0], rh.at[0])
    xf[...] = xraw[...].astype(F32)
    first = jnp.logical_and(z == 0, core == 0)
    xf[0:64, :] = jnp.where(first, jnp.zeros((64, 128), F32), xf[0:64, :])
    xpf[:, 0:128] = xf[pl.ds(0, 800, stride=2), :]
    xpf[:, 128:256] = xf[pl.ds(1, 800, stride=2), :]
    for s in range(16):
        rows = 800 if s == 0 else 784
        xs[s, 0:rows, :] = xpf[pl.ds(s, rows), :].astype(BF)

    acc[...] = jnp.zeros_like(acc)

    def shifted(kappa):
        e = 32 - kappa
        s = lax.rem(e, 16)
        return xs[s, pl.ds(pl.multiple_of(e - s, 16), 768), :]

    def forward_chunk(zc):
        lag = zc * 8
        before = wbuf[lax.rem(lag + 63, 64)]
        before = jnp.where(zc == 0, jnp.zeros_like(before), before)
        left, right = [], []
        for d in range(4):
            low = wbuf[lag + 2 * d]
            prior = before if d == 0 else wbuf[lag + 2 * d - 1]
            high = wbuf[lag + 2 * d + 1]
            left.append(shifted(4 * zc + d))
            right.append(jnp.concatenate([jnp.concatenate([low, prior], 1), jnp.concatenate([high, low], 1)], 0))
        acc[...] += lax.dot_general(jnp.concatenate(left, 1), jnp.concatenate(right, 1), (((1,), (1,)), ((), ())),
                                    preferred_element_type=F32)

    for step in range(1, 5):
        for way, sub in ((0, 0), (1, 1), (0, 1), (1, 0)):
            if step == 4 and way != sub:
                continue
            ring_got(way, step, sub)
            if step < 3 or (step == 3 and way == sub):
                go(ring_send(way, step, sub))
            go(pair_send(2 * step - 1 + (way if step < 4 else 0), z - step if way == 0 else z + step, sub))
        if step == 1:
            for sub in range(2):
                pair_got(0, z, sub)
        for way, sub in ((0, 0), (1, 1), (0, 1), (1, 0)):
            if step == 4 and way != sub:
                continue
            pair_got(2 * step - 1 + (way if step < 4 else 0), z - step if way == 0 else z + step, sub)

        @pl.loop(0, 2)
        def _(i):
            forward_chunk(lax.rem(z + 8 + step - i * (2 * step - 1), 8))
    acc[:, 0:128] += lax.dot_general(xs[0, 0:768, 128:256], wbuf[63], (((1,), (1,)), ((), ())),
                                     preferred_element_type=F32)

    for k in (1, 2, 3):
        j = lax.rem(q + k, 4)
        csend[k - 1] = acc[pl.ds(pl.multiple_of(192 * j, 64), 192), :].astype(BF)
        go(send(csend.at[k - 1], crecv.at[3 - k], sc.at[k - 1], rc.at[3 - k], peer(j)))
    got(mraw, sm.at[0], rm.at[0])
    got(lraw, sm.at[1], rm.at[1])
    mf[...] = mraw[...].astype(F32)
    mine = pl.ds(pl.multiple_of(192 * q, 64), 192)
    total = acc[mine, :]
    for k in range(3):
        got(crecv.at[k], sc.at[k], rc.at[k])
        total = total + crecv[k].astype(F32)
    limit = lraw[0:1, :]
    for i in range(2):
        when = (2 * lax.broadcasted_iota(jnp.int32, (192, 128), 0) + i).astype(F32)
        gap = mf[pl.ds(i, 192, stride=2), :] - total[:, i * 128:(i + 1) * 128] * (1.0 / math.sqrt(LAGS * M))
        kept = jnp.where(when < limit, gap, 0.0).astype(BF)
        rall[mine, i * 128:(i + 1) * 128] = kept
        mf[pl.ds(i, 192, stride=2), :] = kept.astype(F32)
    for k in (1, 2, 3):
        go(send(rall.at[mine], rall.at[mine], sr.at[k - 1], rr.at[3 - k], peer(lax.rem(q + k, 4))))
    rout[...] = mf[...].astype(BF)
    start_any(rout, rres, sm.at[2], rm.at[2], t_in(q))
    for k in range(3):
        got(rall.at[pl.ds(pl.multiple_of(192 * lax.rem(q + k + 1, 4), 64), 192)], sr.at[k], rr.at[k])
    rt[...] = rall[...].astype(F32).T.astype(BF)

    def ring_add(step, way, sub):
        slot = 2 * step - (1 if way == 0 and step > 0 else 0)
        own = dall[slot, pl.ds(core * 4 + 2 * sub, 2)]
        own = own + dxr[slot, pl.ds(2 * sub, 2)].astype(F32)
        if step > (0 if way == sub else 1):
            got(gr.at[way, step - 1, sub], sg.at[way, step - 1, sub], rg.at[way, step - 1, sub])
            own = own + gr[way, step - 1, sub].astype(F32)
        gs[way, step, sub] = own.astype(BF)
        return send(gs.at[way, step, sub], gr.at[way, step, sub], sg.at[way, step, sub], rg.at[way, step, sub],
                    along(1 if way == 0 else -1))

    @pl.loop(0, 8)
    def _(pos):
        m = (pos + 1) // 2
        zc = lax.rem(z + 8 + (4 - m) * (2 * (pos % 2) - 1), 8)
        blocks = []
        for d in range(4):
            blocks.append(jnp.dot(rt[...], shifted(4 * zc + d), preferred_element_type=F32))
            if d > 0:
                dall[pos, 2 * d - 1] = blocks[d - 1][128:, :128] + blocks[d][:128, 128:]
            dall[pos, 2 * d] = blocks[d][:128, :128] + blocks[d][128:, 128:]
        last = jnp.dot(rt[0:128, :], shifted(4 * zc + 4)[:, 128:256], preferred_element_type=F32)
        dall[pos, 7] = blocks[3][128:, :128] + last
        dxs[pos] = dall[pos, pl.ds((1 - core) * 4, 4)].astype(BF)
        send(dxs.at[pos], dxr.at[pos], sdx.at[pos], rdx.at[pos], partner).start()
        for step in range(4):
            @pl.when(pos == 2 * step)
            def _():
                for slot in ((2 * step - 1, 2 * step) if step else (0,)):
                    got(dxr.at[slot], sdx.at[slot], rdx.at[slot])
                for way, sub in ((0, 0), (1, 1), (0, 1), (1, 0)):
                    if step or way == sub:
                        ring_add(step, way, sub).start()

    got(dxr.at[7], sdx.at[7], rdx.at[7])
    for sub in range(2):
        whole = dall[7, pl.ds(core * 4 + 2 * sub, 2)] + dxr[7, pl.ds(2 * sub, 2)].astype(F32)
        for way in range(2):
            got(gr.at[way, 3, sub], sg.at[way, 3, sub], rg.at[way, 3, sub])
            whole = whole + gr[way, 3, sub].astype(F32)
        fs[pl.ds(2 * sub, 2)] = whole.astype(BF)
        for j in (2 * sub, 2 * sub + 1):
            start_any(fs.at[j], fr.at[q], sf.at[j], rf.at[q], t_in(j))

    got(rres, sm.at[2], rm.at[2])
    res_ref[...] = rres[...]
    for c in range(4):
        got(fr.at[c], sf.at[c], rf.at[c])
        cols = slice(c * 128, (c + 1) * 128)
        new_ref[:, cols] = par_ref[:, cols] + fr[c].astype(F32) * (0.5 / math.sqrt(24576))

    for desc in sent:
        desc.wait_send()
    for c in range(4):
        done_any(wsend.at[c], wbuf.at[tm], sb1.at[c], rb1.at[x], t_out(c))
        done_any(rec_ref, xraw.at[own_rows], sa.at[c], ra.at[x], spread(c))
        done_any(fs.at[c], fr.at[q], sf.at[c], rf.at[q], t_in(c))
    done_any(meas_ref, mraw, sm.at[0], rm.at[0], t_out(x))
    done_any(lsend, lraw, sm.at[1], rm.at[1], t_out(x))
    done_any(rout, rres, sm.at[2], rm.at[2], t_in(q))

    @pl.loop(0, 8)
    def _(pos):
        send(dxs.at[pos], dxr.at[pos], sdx.at[pos], rdx.at[pos], partner).wait_send()
    for step in range(4):
        for way in range(2):
            for sub in range(2):
                if step or way == sub:
                    send(gs.at[way, step, sub], gr.at[way, step, sub], sg.at[way, step, sub], rg.at[way, step, sub],
                         along(1 if way == 0 else -1)).wait_send()


def on_device(records, measured, markov_params, seg_lengths):
    dma = pltpu.SemaphoreType.DMA
    new, res = pl.pallas_call(
        body,
        out_shape=(jax.ShapeDtypeStruct((128, 512), F32), jax.ShapeDtypeStruct((384, 128), BF)),
        in_specs=[pl.BlockSpec(memory_space=pltpu.SMEM)] + [pl.BlockSpec(memory_space=pltpu.VMEM)] * 3,
        out_specs=(pl.BlockSpec(memory_space=pltpu.VMEM), pl.BlockSpec(memory_space=pltpu.VMEM)),
        scratch_shapes=[
            pltpu.VMEM((4, 128, 128), BF),
            pltpu.VMEM((64, 128, 128), BF),
            pltpu.VMEM((1600, 128), BF),
            pltpu.VMEM((1600, 128), F32),
            pltpu.VMEM((800, 256), F32),
            pltpu.VMEM((16, 800, 256), BF),
            pltpu.VMEM((8, 128), F32),
            pltpu.VMEM((8, 128), F32),
            pltpu.VMEM((384, 128), BF),
            pltpu.VMEM((384, 128), F32),
            pltpu.VMEM((768, 256), F32),
            pltpu.VMEM((3, 192, 256), BF),
            pltpu.VMEM((3, 192, 256), BF),
            pltpu.VMEM((768, 256), BF),
            pltpu.VMEM((256, 768), BF),
            pltpu.VMEM((384, 128), BF),
            pltpu.VMEM((384, 128), BF),
            pltpu.VMEM((8, 8, 128, 128), F32),
            pltpu.VMEM((8, 4, 128, 128), BF),
            pltpu.VMEM((8, 4, 128, 128), BF),
            pltpu.VMEM((2, 4, 2, 2, 128, 128), BF),
            pltpu.VMEM((2, 4, 2, 2, 128, 128), BF),
            pltpu.VMEM((4, 128, 128), BF),
            pltpu.VMEM((4, 128, 128), BF),
            dma((4,)), dma((4,)), dma((4,)), dma((4,)), dma((3,)), dma((3,)), dma((1,)), dma((1,)),
            dma((2, 4, 2)), dma((2, 4, 2)), dma((8, 2)), dma((8, 2)), dma((3,)), dma((3,)), dma((3,)), dma((3,)),
            dma((8,)), dma((8,)), dma((2, 4, 2)), dma((2, 4, 2)), dma((4,)), dma((4,)),
        ],
        compiler_params=pltpu.CompilerParams(collective_id=0, has_side_effects=True, vmem_limit_bytes=56 * 1024 * 1024),
        name="gradient_step",
    )(seg_lengths, records, measured, markov_params.reshape(128, 512))
    return new.reshape(1, 128, 512), res


def solution(mesh):
    in_specs = (P("tm", "grp"), P("tm", "grp"), P("tm", "grp", None), P("tm"))
    out_specs = (P("tm", "grp", None), P("tm", "grp"))
    return jax.shard_map(on_device, mesh=mesh, in_specs=in_specs, out_specs=out_specs, check_vma=False)
```

```python
import math

import jax
import jax.numpy as jnp
from jax import lax
from jax.experimental import pallas as pl
from jax.experimental.pallas import tpu as pltpu
from jax.sharding import PartitionSpec as P

M = 512
LAGS = 64
BF = jnp.bfloat16
F32 = jnp.float32
HALO = 128
SPAN = 1536


def body(len_ref, rec_ref, meas_ref, par_ref, new_ref, res_ref, wsend, wbuf, xbuf, xt, msend, mrecv, mtf, mtime, lsend,
         lraw, acc, cbuf, ubuf, rp, wq, qq, qs, rsend, rrecv, dall, dxs, dxr, gs, gr, fs, fr,
         sb1, rb1, sa, sa2, sb2, ra, sm, rm, sl, rl, so, ro, sh, rh, sring, rring, spair, rpair, sdx, rdx, sg, rg, sf, rf):
    tm = lax.axis_index("tm")
    grp = lax.axis_index("grp")
    z = tm // 8
    yh = (tm // 4) % 2
    x = tm % 4
    yl = grp // 2
    core = grp % 2
    q = yl * 2 + yh
    home = yh == core

    def spread(j):
        return z * 8 + core * 4 + j, yl * 2 + yh

    def along(step):
        return lax.rem(z + step + 8, 8) * 8 + yh * 4 + x, grp

    def over_x(k):
        return z * 8 + yh * 4 + lax.rem(x + k, 4), grp

    def over_y(k):
        j = lax.rem(q + k, 4)
        return z * 8 + (j % 2) * 4 + x, (j // 2) * 2 + core

    partner = (tm, yl * 2 + 1 - core)
    ahead = (lax.rem(z + core, 8) * 8 + yh * 4 + x, yl * 2 + 1 - core)
    behind = (lax.rem(z + core + 7, 8) * 8 + yh * 4 + x, yl * 2 + 1 - core)

    def first_hop(j):
        xj = core * x + (1 - core) * j
        yhj = core * (j % 2) + (1 - core) * yh
        ylj = core * (j // 2) + (1 - core) * yl
        return z * 8 + yhj * 4 + xj, ylj * 2 + yh

    def hop_from(j, c):
        if c == 0:
            return z * 8 + yh * 4 + j, yl * 2
        return z * 8 + core * 4 + x, j * 2 + 1

    def is_me(dev):
        return jnp.logical_and(dev[0] == tm, dev[1] == grp)

    def where(dev):
        return dict(device_id={"tm": dev[0], "grp": dev[1]}, device_id_type=pl.DeviceIdType.MESH)

    def send(src, dst, ssem, rsem, dev):
        return pltpu.make_async_remote_copy(src_ref=src, dst_ref=dst, send_sem=ssem, recv_sem=rsem, **where(dev))

    sent = []

    def go(src, dst, ssem, rsem, dev, only=None):
        desc = send(src, dst, ssem, rsem, dev)
        if only is None:
            desc.start()
            sent.append(desc.wait_send)
            return

        @pl.when(only)
        def _():
            desc.start()

        def wait():
            @pl.when(only)
            def _():
                send(src, dst, ssem, rsem, dev).wait_send()
        sent.append(wait)

    def go_any(src, dst, ssem, rsem, dev):
        me = is_me(dev)

        @pl.when(me)
        def _():
            pltpu.make_async_copy(src, dst, rsem).start()
        go(src, dst, ssem, rsem, dev, jnp.logical_not(me))

    def got(dst, ssem, rsem):
        send(dst, dst, ssem, rsem, partner).wait_recv()

    barrier = pltpu.get_barrier_semaphore()
    count = jnp.int32(0)
    friends = [(spread(j), True) for j in range(4)] + [(first_hop(j), True) for j in range(4)]
    friends += [(hop_from(j, 0), home) for j in range(4)] + [(hop_from(j, 1), True) for j in range(2)]
    for n, (dev, holds) in enumerate(friends):
        other = jnp.logical_and(jnp.logical_not(is_me(dev)), holds)
        count = count + other.astype(jnp.int32)

        @pl.when(other)
        def _():
            pl.semaphore_signal(barrier, inc=1, **where(dev))
    sure = [over_x(k) for k in (1, 2, 3)] + [over_y(k) for k in (1, 2, 3)]
    sure += [along(1), along(-1), partner, ahead, behind]
    for dev in sure:
        pl.semaphore_signal(barrier, inc=1, **where(dev))
    wsend[...] = par_ref[...].astype(BF)
    lsend[...] = jnp.full((8, 128), len_ref[0], jnp.int32).astype(F32)
    msend[...] = meas_ref[...].astype(F32).T.astype(BF)
    xbuf[0:64, :] = jnp.zeros((64, 512), BF)
    mtf[32:128, :] = jnp.zeros((96, SPAN), F32)
    rp[...] = jnp.zeros_like(rp)
    acc[...] = jnp.zeros_like(acc)
    pl.semaphore_wait(barrier, count + len(sure))

    def lag_rows(chunk, half, sub):
        return wbuf.at[pl.ds(pl.multiple_of(lax.rem(chunk + 8, 8) * 256 + half * 128 + sub * 32, 32), 32)]

    def slot(g, j):
        return xbuf.at[pl.ds(pl.multiple_of(HALO + 384 * j, 128), 384), pl.ds(pl.multiple_of(128 * g, 128), 128)]

    for j in range(4):
        go_any(wsend.at[pl.ds(32 * j, 32)], lag_rows(z, yh, x), sb1.at[j], rb1.at[x], spread(j))
    for j in range(4):
        go_any(rec_ref, slot(grp, x), sa.at[j], ra.at[grp * 4 + x], first_hop(j))

    def ring_send(way, step, sub):
        ref = lag_rows(z - step if way == 0 else z + step, core, sub)
        go(ref, ref, sring.at[way, step, sub], rring.at[way, step, sub], along(1 if way == 0 else -1))

    def ring_got(way, step, sub):
        ref = lag_rows(z - step if way == 0 else z + step, core, sub)
        got(ref, sring.at[way, step - 1, sub], rring.at[way, step - 1, sub])

    def pair_send(n, chunk, sub):
        ref = lag_rows(chunk, core, sub)
        go(ref, ref, spair.at[n, sub], rpair.at[n, sub], partner)

    def pair_got(n, chunk, sub):
        got(lag_rows(chunk, 1 - core, sub), spair.at[n, sub], rpair.at[n, sub])

    def number(way, step):
        return 2 * step - 1 + (way if step < 4 else 0)

    for sub in range(4):
        got(lag_rows(z, core, sub), sb1.at[sub], rb1.at[sub])
        ring_send(0, 0, sub)
        ring_send(1, 0, sub)
        pair_send(0, z, sub)

    def slot_got(g, j):
        got(slot(g, j), sa.at[0], ra.at[g * 4 + j])

    def turned(g, j):
        cols = pl.ds(pl.multiple_of(HALO + 384 * j, 128), 384)
        rows = pl.ds(pl.multiple_of(128 * g, 128), 128)
        xt[rows, cols] = xbuf[cols, rows].T

    for n in range(2):
        g = 2 * n + 1
        slot_got(g, x)
        for k in (1, 2, 3):
            go(slot(g, x), slot(g, x), sb2.at[n, k - 1], ra.at[g * 4 + x], over_x(k))
    for j in range(4):
        @pl.when(home)
        def _():
            slot_got(yl * 2, j)
        for k in (1, 2, 3):
            go(slot(yl * 2, j), slot(yl * 2, j), sa2.at[j, k - 1], ra.at[yl * 8 + j], over_y(k), home)
    for j in range(4):
        go_any(msend.at[pl.ds(32 * j, 32)], mrecv.at[x], sm.at[j], rm.at[x], spread(j))
        go_any(lsend, lraw.at[x], sl.at[j], rl.at[x], spread(j))

    ways = ((0, (0, 1)), (1, (2, 3)), (0, (2, 3)), (1, (0, 1)))
    for step in range(1, 5):
        for n, (way, subs) in enumerate(ways):
            if step == 4 and n >= 2:
                continue
            for sub in subs:
                ring_got(way, step, sub)
                if step < 3 or (step == 3 and n < 2):
                    ring_send(way, step, sub)
                pair_send(number(way, step), z - step if way == 0 else z + step, sub)
        if step == 2:
            for j in range(4):
                got(mrecv.at[j], sm.at[j], rm.at[j])
                got(lraw.at[j], sl.at[j], rl.at[j])
                mtf[0:32, 384 * j:384 * (j + 1)] = mrecv[j].astype(F32)
            mtime[...] = mtf[...].T
            for n in range(2):
                turned(2 * n + 1, x)
            for j in range(4):
                @pl.when(jnp.logical_not(home))
                def _():
                    slot_got(yl * 2, j)
                turned(yl * 2, j)
        if step == 3:
            for j in range(4):
                g = 2 * (1 - yl)
                slot_got(g, j)
                turned(g, j)
    for k in (1, 3, 2):
        for n in range(2):
            j = lax.rem(x + k, 4)
            slot_got(2 * n + 1, j)
            turned(2 * n + 1, j)
    last_rows = xbuf.at[pl.ds(HALO + SPAN - 64, 64)]
    halo_rows = xbuf.at[pl.ds(HALO - 64, 64)]
    go(last_rows, halo_rows, sh.at[0], rh.at[0], ahead)
    for sub in range(4):
        pair_got(0, z, sub)
    for step in range(1, 5):
        for n, (way, subs) in enumerate(ways):
            if step == 4 and n >= 2:
                continue
            for sub in subs:
                pair_got(number(way, step), z - step if way == 0 else z + step, sub)
    got(halo_rows, sh.at[0], rh.at[0])
    first = jnp.logical_and(z == 0, core == 0)
    halo = xbuf[HALO - 64:HALO, :]
    halo = jnp.where(first, jnp.zeros_like(halo), halo)
    xbuf[HALO - 64:HALO, :] = halo
    xt[:, 0:HALO] = xbuf[0:HALO, :].T

    @pl.loop(0, 8)
    def _(c):
        w = wbuf[pl.ds(pl.multiple_of(c * 256, 256), 256), :]

        @pl.loop(0, 4)
        def _(i):
            part = lax.dot_general(xbuf[pl.ds(pl.multiple_of(64 + 400 * i, 16), 400), :], w, (((1,), (1,)), ((), ())),
                                   preferred_element_type=F32)
            acc[pl.ds(pl.multiple_of(400 * i + 8 * c, 8), 400), :] += part

    cbuf[...] = acc[48:1600, 0:128] + acc[44:1596, 128:256]
    ubuf[...] = cbuf[8:1552, :] + pltpu.roll(cbuf[6:1550, :], 64, 1)
    lane = lax.broadcasted_iota(jnp.int32, (384, 128), 1)
    row = lax.broadcasted_iota(jnp.int32, (384, 128), 0).astype(F32)
    for j in range(4):
        lo = 384 * j
        total = ubuf[lo + 8:lo + 392, :] + pltpu.roll(ubuf[lo + 7:lo + 391, :], 96, 1)
        gap = mtime[lo:lo + 384, :] - total * (1.0 / math.sqrt(LAGS * M))
        keep = jnp.logical_and(row < lraw[j, 0:1, :], lane < 32)
        rp[HALO + lo:HALO + lo + 384, :] = jnp.where(keep, gap, 0.0).astype(BF).astype(F32)
    wq[...] = rp[0:1736, :] + pltpu.roll(rp[1:1737, :], 32, 1)
    qq[...] = wq[0:1732, :] + pltpu.roll(wq[2:1734, :], 64, 1)
    for n in range(2):
        qs[n, :, 0:128] = qq[8 * n:8 * n + 1712, :].astype(BF)
        qs[n, :, 128:256] = qq[8 * n + 4:8 * n + 1716, :].astype(BF)

    def ring_add(step, way, sub):
        at = 2 * step - (1 if way == 0 and step > 0 else 0)
        rows = pl.ds(128 * sub, 128)
        own = dall[at, core, rows, :] + dxr[at, rows, :].astype(F32)
        early = (sub < 2) == (way == 0)
        if step > (0 if early else 1):
            got(gr.at[way, step - 1, sub], sg.at[way, step - 1, sub], rg.at[way, step - 1, sub])
            own = own + gr[way, step - 1, sub].astype(F32)
        gs[way, step, sub] = own.astype(BF)
        return send(gs.at[way, step, sub], gr.at[way, step, sub], sg.at[way, step, sub], rg.at[way, step, sub],
                    along(1 if way == 0 else -1))

    @pl.loop(0, 8)
    def _(pos):
        m = (pos + 1) // 2
        zc = lax.rem(z + 8 + (4 - m) * (2 * (pos % 2) - 1), 8)
        odd = zc % 2
        part = jnp.dot(xt[...], qs[odd, pl.ds(pl.multiple_of(8 * (zc - odd), 16), HALO + SPAN), :],
                       preferred_element_type=F32)
        dall[pos, 0] = part[:, 0:128]
        dall[pos, 1] = part[:, 128:256]
        dxs[pos] = dall[pos, 1 - core].astype(BF)
        send(dxs.at[pos], dxr.at[pos], sdx.at[pos], rdx.at[pos], partner).start()
        for step in range(4):
            @pl.when(pos == 2 * step)
            def _():
                for at in ((2 * step - 1, 2 * step) if step else (0,)):
                    got(dxr.at[at], sdx.at[at], rdx.at[at])
                for n, (way, subs) in enumerate(ways):
                    if step or n < 2:
                        for sub in subs:
                            ring_add(step, way, sub).start()

    back = rp[HALO:HALO + SPAN, :].T
    for j in range(4):
        rsend[j] = back[0:32, 384 * j:384 * (j + 1)].astype(BF)
        go_any(rsend.at[j], rrecv.at[pl.ds(pl.multiple_of(32 * x, 32), 32)], so.at[j], ro.at[x], spread(j))
    for j in range(4):
        got(rrecv.at[pl.ds(32 * j, 32)], so.at[j], ro.at[j])
    res_ref[...] = rrecv[...].astype(F32).T.astype(BF)

    got(dxr.at[7], sdx.at[7], rdx.at[7])
    for sub in range(4):
        rows = pl.ds(128 * sub, 128)
        whole = dall[7, core, rows, :] + dxr[7, rows, :].astype(F32)
        for way in range(2):
            got(gr.at[way, 3, sub], sg.at[way, 3, sub], rg.at[way, 3, sub])
            whole = whole + gr[way, 3, sub].astype(F32)
        fs[:, 128 * sub:128 * (sub + 1)] = whole.T.astype(BF)
    for j in range(4):
        go_any(fs.at[pl.ds(32 * j, 32)], fr.at[pl.ds(pl.multiple_of(32 * x, 32), 32)], sf.at[j], rf.at[x], spread(j))
    for j in range(4):
        rows = pl.ds(32 * j, 32)
        got(fr.at[rows], sf.at[j], rf.at[j])
        new_ref[rows, :] = par_ref[rows, :] + fr[rows, :].astype(F32) * (0.5 / math.sqrt(24576))

    for wait in sent:
        wait()

    @pl.loop(0, 8)
    def _(pos):
        send(dxs.at[pos], dxr.at[pos], sdx.at[pos], rdx.at[pos], partner).wait_send()
    for step in range(4):
        for n, (way, subs) in enumerate(ways):
            if step or n < 2:
                for sub in subs:
                    send(gs.at[way, step, sub], gr.at[way, step, sub], sg.at[way, step, sub], rg.at[way, step, sub],
                         along(1 if way == 0 else -1)).wait_send()


def on_device(records, measured, markov_params, seg_lengths):
    dma = pltpu.SemaphoreType.DMA
    new, res = pl.pallas_call(
        body,
        out_shape=(jax.ShapeDtypeStruct((128, 512), F32), jax.ShapeDtypeStruct((384, 128), BF)),
        in_specs=[pl.BlockSpec(memory_space=pltpu.SMEM)] + [pl.BlockSpec(memory_space=pltpu.VMEM)] * 3,
        out_specs=(pl.BlockSpec(memory_space=pltpu.VMEM), pl.BlockSpec(memory_space=pltpu.VMEM)),
        scratch_shapes=[
            pltpu.VMEM((128, 512), BF),
            pltpu.VMEM((2048, 512), BF),
            pltpu.VMEM((HALO + SPAN, 512), BF),
            pltpu.VMEM((512, HALO + SPAN), BF),
            pltpu.VMEM((128, 384), BF),
            pltpu.VMEM((4, 32, 384), BF),
            pltpu.VMEM((128, SPAN), F32),
            pltpu.VMEM((SPAN, 128), F32),
            pltpu.VMEM((8, 128), F32),
            pltpu.VMEM((4, 8, 128), F32),
            pltpu.VMEM((1664, 256), F32),
            pltpu.VMEM((1552, 128), F32),
            pltpu.VMEM((1544, 128), F32),
            pltpu.VMEM((1744, 128), F32),
            pltpu.VMEM((1736, 128), F32),
            pltpu.VMEM((1732, 128), F32),
            pltpu.VMEM((2, 1712, 256), BF),
            pltpu.VMEM((4, 32, 384), BF),
            pltpu.VMEM((128, 384), BF),
            pltpu.VMEM((8, 2, 512, 128), F32),
            pltpu.VMEM((8, 512, 128), BF),
            pltpu.VMEM((8, 512, 128), BF),
            pltpu.VMEM((2, 4, 4, 128, 128), BF),
            pltpu.VMEM((2, 4, 4, 128, 128), BF),
            pltpu.VMEM((128, 512), BF),
            pltpu.VMEM((128, 512), BF),
            dma((4,)), dma((4,)), dma((4,)), dma((4, 3)), dma((2, 3)), dma((16,)), dma((4,)), dma((4,)), dma((4,)), dma((4,)),
            dma((4,)), dma((4,)), dma((1,)), dma((1,)),
            dma((2, 4, 4)), dma((2, 4, 4)), dma((8, 4)), dma((8, 4)),
            dma((8,)), dma((8,)), dma((2, 4, 4)), dma((2, 4, 4)), dma((4,)), dma((4,)),
        ],
        compiler_params=pltpu.CompilerParams(collective_id=0, has_side_effects=True, vmem_limit_bytes=56 * 1024 * 1024),
        name="gradient_step",
    )(seg_lengths, records, measured, markov_params.reshape(128, 512))
    return new.reshape(1, 128, 512), res


def solution(mesh):
    in_specs = (P("tm", "grp"), P("tm", "grp"), P("tm", "grp", None), P("tm"))
    out_specs = (P("tm", "grp", None), P("tm", "grp"))
    return jax.shard_map(on_device, mesh=mesh, in_specs=in_specs, out_specs=out_specs, check_vma=False)
```

```python
import math

import jax
import jax.numpy as jnp
from jax import lax
from jax.experimental import pallas as pl
from jax.experimental.pallas import tpu as pltpu
from jax.sharding import PartitionSpec as P

M = 512
LAGS = 64
BF = jnp.bfloat16
F32 = jnp.float32
HALO = 128
SPAN = 1536


def body(len_ref, rec_ref, meas_ref, par_ref, new_ref, res_ref, wsend, wbuf, xbuf, xt, msend, mrecv, mtf, mtime, lsend,
         lraw, acc, cbuf, ubuf, rp, wq, qq, qs, rsend, rrecv, dall, dxs, dxr, gs, gr, fs, fr,
         sb1, rb1, sa, sa2, sb2, ra, sm, rm, sl, rl, so, ro, sh, rh, sring, rring, spair, rpair, sdx, rdx, sg, rg, sf, rf):
    tm = lax.axis_index("tm")
    grp = lax.axis_index("grp")
    z = tm // 8
    yh = (tm // 4) % 2
    x = tm % 4
    yl = grp // 2
    core = grp % 2
    q = yl * 2 + yh
    home = yh == core

    def spread(j, dz=0):
        return lax.rem(z + dz + 8, 8) * 8 + core * 4 + j, yl * 2 + yh

    def along(step):
        return lax.rem(z + step + 8, 8) * 8 + yh * 4 + x, grp

    def over_x(k):
        return z * 8 + yh * 4 + lax.rem(x + k, 4), grp

    def over_y(k):
        j = lax.rem(q + k, 4)
        return z * 8 + (j % 2) * 4 + x, (j // 2) * 2 + core

    partner = (tm, yl * 2 + 1 - core)
    ahead = (lax.rem(z + core, 8) * 8 + yh * 4 + x, yl * 2 + 1 - core)
    behind = (lax.rem(z + core + 7, 8) * 8 + yh * 4 + x, yl * 2 + 1 - core)

    def first_hop(j):
        xj = core * x + (1 - core) * j
        yhj = core * (j % 2) + (1 - core) * yh
        ylj = core * (j // 2) + (1 - core) * yl
        return z * 8 + yhj * 4 + xj, ylj * 2 + yh

    def hop_from(j, c):
        if c == 0:
            return z * 8 + yh * 4 + j, yl * 2
        return z * 8 + core * 4 + x, j * 2 + 1

    def is_me(dev):
        return jnp.logical_and(dev[0] == tm, dev[1] == grp)

    def where(dev):
        return dict(device_id={"tm": dev[0], "grp": dev[1]}, device_id_type=pl.DeviceIdType.MESH)

    def send(src, dst, ssem, rsem, dev):
        return pltpu.make_async_remote_copy(src_ref=src, dst_ref=dst, send_sem=ssem, recv_sem=rsem, **where(dev))

    sent = []

    def go(src, dst, ssem, rsem, dev, only=None):
        if only is None:
            send(src, dst, ssem, rsem, dev).start()
            sent.append(lambda: send(src, dst, ssem, rsem, dev).wait_send())
            return

        @pl.when(only)
        def _():
            send(src, dst, ssem, rsem, dev).start()

        def wait():
            @pl.when(only)
            def _():
                send(src, dst, ssem, rsem, dev).wait_send()
        sent.append(wait)

    def go_any(src, dst, ssem, rsem, dev):
        me = is_me(dev)

        @pl.when(me)
        def _():
            pltpu.make_async_copy(src, dst, rsem).start()
        go(src, dst, ssem, rsem, dev, jnp.logical_not(me))

    def got(dst, ssem, rsem):
        send(dst, dst, ssem, rsem, partner).wait_recv()

    barrier = pltpu.get_barrier_semaphore()
    count = jnp.int32(0)
    friends = [(spread(j, dz), True) for dz in (1, -1) for j in range(4)] + [(spread(j), True) for j in range(4)] + [(first_hop(j), True) for j in range(4)]
    friends += [(hop_from(j, 0), home) for j in range(4)] + [(hop_from(j, 1), True) for j in range(2)]
    for n, (dev, holds) in enumerate(friends):
        other = jnp.logical_and(jnp.logical_not(is_me(dev)), holds)
        count = count + other.astype(jnp.int32)

        @pl.when(other)
        def _():
            pl.semaphore_signal(barrier, inc=1, **where(dev))
    sure = [over_x(k) for k in (1, 2, 3)] + [over_y(k) for k in (1, 2, 3)]
    sure += [along(1), along(-1), partner, ahead, behind]
    for dev in sure:
        pl.semaphore_signal(barrier, inc=1, **where(dev))
    wsend[...] = par_ref[...].astype(BF)
    lsend[...] = jnp.full((8, 128), len_ref[0], jnp.int32).astype(F32)
    pl.semaphore_wait(barrier, count + len(sure))

    def lag_rows(chunk, half, sub):
        return wbuf.at[pl.ds(pl.multiple_of(lax.rem(chunk + 8, 8) * 256 + half * 128 + sub * 32, 32), 32)]

    def slot(g, j):
        return xbuf.at[pl.ds(pl.multiple_of(HALO + 384 * j, 128), 384), pl.ds(pl.multiple_of(128 * g, 128), 128)]

    for j in range(4):
        go_any(wsend.at[pl.ds(32 * j, 32)], lag_rows(z, yh, x), sb1.at[j], rb1.at[x], spread(j))
    for j in range(4):
        go_any(rec_ref, slot(grp, x), sa.at[j], ra.at[grp * 4 + x], first_hop(j))

    msend[...] = meas_ref[...].astype(F32).T.astype(BF)
    for j in range(4):
        go_any(msend.at[pl.ds(32 * j, 32)], mrecv.at[x], sm.at[j], rm.at[x], spread(j))
        go_any(lsend, lraw.at[x], sl.at[j], rl.at[x], spread(j))
    xbuf[0:64, :] = jnp.zeros((64, 512), BF)
    mtf[32:128, :] = jnp.zeros((96, SPAN), F32)
    rp[...] = jnp.zeros_like(rp)
    acc[...] = jnp.zeros_like(acc)

    def ring_send(way, step, sub):
        ref = lag_rows(z - step if way == 0 else z + step, core, sub)
        go(ref, ref, sring.at[way, step, sub], rring.at[way, step, sub], along(1 if way == 0 else -1))

    def ring_got(way, step, sub):
        ref = lag_rows(z - step if way == 0 else z + step, core, sub)
        got(ref, sring.at[way, step - 1, sub], rring.at[way, step - 1, sub])

    def pair_copy(way, step, sub):
        ref = lag_rows(z - step if way == 0 else z + step, core, sub)
        n = number(way, step)
        return send(ref, ref, spair.at[n, sub], rpair.at[n, sub], partner)

    def pair_send(way, step, sub):
        pair_copy(way, step, sub).start()
        sent.append(lambda: pair_copy(way, step, sub).wait_send())

    def pair_got(n, chunk, sub):
        got(lag_rows(chunk, 1 - core, sub), spair.at[n, sub], rpair.at[n, sub])

    def number(way, step):
        return 2 * step - 1 + (way if step < 4 else 0) if step else 0

    for sub in range(4):
        got(lag_rows(z, core, sub), sb1.at[sub], rb1.at[sub])
        ring_send(0, 0, sub)
        ring_send(1, 0, sub)
        pair_send(0, 0, sub)

    def slot_got(g, j):
        got(slot(g, j), sa.at[0], ra.at[g * 4 + j])

    def turned(g, j):
        cols = pl.ds(pl.multiple_of(HALO + 384 * j, 128), 384)
        rows = pl.ds(pl.multiple_of(128 * g, 128), 128)
        xt[rows, cols] = xbuf[cols, rows].T

    for n in range(2):
        g = 2 * n + 1
        slot_got(g, x)
        for k in (1, 2, 3):
            go(slot(g, x), slot(g, x), sb2.at[n, k - 1], ra.at[g * 4 + x], over_x(k))
    for n in range(4):
        j = lax.rem(x + 4 - n, 4)

        @pl.when(home)
        def _():
            slot_got(yl * 2, j)
        for k in (1, 2, 3):
            go(slot(yl * 2, j), slot(yl * 2, j), sa2.at[n, k - 1], ra.at[yl * 8 + j], over_y(k), home)

    def arrived(n):
        j = lax.rem(x + 4 - n, 4)

        @pl.when(jnp.logical_not(home))
        def _():
            slot_got(yl * 2, j)
        slot_got(2 * (1 - yl), j)
        for g in range(4):
            if n and g % 2:
                slot_got(g, j)
            turned(g, j)

    ways = ((0, (0, 1)), (1, (2, 3)), (0, (2, 3)), (1, (0, 1)))
    def passed_on(step):
        for n, (way, subs) in enumerate(ways):
            if step == 4 and n >= 2:
                continue
            for sub in subs:
                ring_got(way, step, sub)
                if step < 3 or (step == 3 and n < 2):
                    ring_send(way, step, sub)
                pair_send(way, step, sub)

    def paired(step):
        for n, (way, subs) in enumerate(ways):
            if step == 4 and n >= 2:
                continue
            for sub in subs:
                pair_got(number(way, step), z - step if way == 0 else z + step, sub)

    halo_rows = xbuf.at[pl.ds(HALO - 64, 64)]
    last_rows = xbuf.at[pl.ds(HALO + SPAN - 64, 64)]

    def forward(c, lo, rows):
        part = lax.dot_general(xbuf[lo:lo + rows, :], wbuf[pl.ds(pl.multiple_of(c * 256, 256), 256), :],
                               (((1,), (1,)), ((), ())), preferred_element_type=F32)
        acc[pl.ds(pl.multiple_of(lo - 64 + 8 * c, 8), rows), :] += part

    for step in range(1, 4):
        passed_on(step)
    for j in range(4):
        got(mrecv.at[j], sm.at[j], rm.at[j])
        got(lraw.at[j], sl.at[j], rl.at[j])
        mtf[0:32, 384 * j:384 * (j + 1)] = mrecv[j].astype(F32)
    mtime[...] = mtf[...].T
    for n in range(4):
        arrived(n)
    go(last_rows, halo_rows, sh.at[0], rh.at[0], ahead)
    for sub in range(4):
        pair_got(0, z, sub)
    for step in range(1, 4):
        paired(step)

    @pl.loop(0, 8)
    def _(i):
        @pl.when(i == 5)
        def _():
            passed_on(4)

        @pl.when(i == 7)
        def _():
            paired(4)
        forward(lax.rem(z + 8 + (1 - 2 * (i % 2)) * ((i + 1) // 2), 8), HALO, SPAN)
    got(halo_rows, sh.at[0], rh.at[0])
    first = jnp.logical_and(z == 0, core == 0)
    halo = xbuf[HALO - 64:HALO, :]
    halo = jnp.where(first, jnp.zeros_like(halo), halo)
    xbuf[HALO - 64:HALO, :] = halo
    xt[:, 0:HALO] = xbuf[0:HALO, :].T

    @pl.loop(0, 8)
    def _(c):
        forward(c, HALO - 64, 64)

    cbuf[...] = acc[48:1600, 0:128] + acc[44:1596, 128:256]
    ubuf[...] = cbuf[8:1552, :] + pltpu.roll(cbuf[6:1550, :], 64, 1)
    lane = lax.broadcasted_iota(jnp.int32, (384, 128), 1)
    row = lax.broadcasted_iota(jnp.int32, (384, 128), 0).astype(F32)
    for j in range(4):
        lo = 384 * j
        total = ubuf[lo + 8:lo + 392, :] + pltpu.roll(ubuf[lo + 7:lo + 391, :], 96, 1)
        gap = mtime[lo:lo + 384, :] - total * (1.0 / math.sqrt(LAGS * M))
        keep = jnp.logical_and(row < lraw[j, 0:1, :], lane < 32)
        rp[HALO + lo:HALO + lo + 384, :] = jnp.where(keep, gap, 0.0).astype(BF).astype(F32)
    wq[...] = rp[0:1736, :] + pltpu.roll(rp[1:1737, :], 32, 1)
    qq[...] = wq[0:1732, :] + pltpu.roll(wq[2:1734, :], 64, 1)
    for n in range(2):
        qs[n, :, 0:128] = qq[8 * n:8 * n + 1712, :].astype(BF)
        qs[n, :, 128:256] = qq[8 * n + 4:8 * n + 1716, :].astype(BF)

    def ring_add(step, way, sub):
        at = 2 * step - (1 if way == 0 and step > 0 else 0)
        rows = pl.ds(128 * sub, 128)
        own = dall[at, core, rows, :] + dxr[at, rows, :].astype(F32)
        early = (sub < 2) == (way == 0)
        if step > (0 if early else 1):
            got(gr.at[way, step - 1, sub], sg.at[way, step - 1, sub], rg.at[way, step - 1, sub])
            own = own + gr[way, step - 1, sub].astype(F32)
        if step == 3:
            deliver(way, sub, own)
            return
        gs[way, step, sub] = own.astype(BF)
        send(gs.at[way, step, sub], gr.at[way, step, sub], sg.at[way, step, sub], rg.at[way, step, sub],
             along(1 if way == 0 else -1)).start()

    def delivery(n, sub, j):
        cols = pl.ds(128 * sub, 128)
        return (fs.at[n, pl.ds(32 * j, 32), cols], fr.at[n, pl.ds(pl.multiple_of(32 * x, 32), 32), cols], sf.at[n, sub, j],
                rf.at[n, sub, x], spread(j, (1, -1, 0)[n]))

    def deliver(n, sub, part):
        fs[n, :, 128 * sub:128 * (sub + 1)] = part.T.astype(BF)
        for j in range(4):
            if n < 2:
                send(*delivery(n, sub, j)).start()
            else:
                go_any(*delivery(n, sub, j))

    def correlate(pos):
        m = (pos + 1) // 2
        zc = lax.rem(z + 8 + (4 - m) * (2 * (pos % 2) - 1), 8)
        odd = zc % 2
        part = jnp.dot(xt[...], qs[odd, pl.ds(pl.multiple_of(8 * (zc - odd), 16), HALO + SPAN), :],
                       preferred_element_type=F32)
        dall[pos, 0] = part[:, 0:128]
        dall[pos, 1] = part[:, 128:256]
        dxs[pos] = dall[pos, 1 - core].astype(BF)
        send(dxs.at[pos], dxr.at[pos], sdx.at[pos], rdx.at[pos], partner).start()

    def ring_step(step):
        for at in ((2 * step - 1, 2 * step) if step else (0,)):
            got(dxr.at[at], sdx.at[at], rdx.at[at])
        for n in (0, 1) if step == 0 else (2, 3, 0, 1) if step == 1 else range(4):
            way, subs = ways[n]
            for sub in subs:
                ring_add(step, way, sub)

    @pl.loop(0, 4)
    def _(pos):
        correlate(pos)
        for step in range(2):
            @pl.when(pos == 2 * step + 1)
            def _():
                ring_step(step)

    back = rp[HALO:HALO + SPAN, :].T
    for j in range(4):
        rsend[j] = back[0:32, 384 * j:384 * (j + 1)].astype(BF)
        go_any(rsend.at[j], rrecv.at[pl.ds(pl.multiple_of(32 * x, 32), 32)], so.at[j], ro.at[x], spread(j))

    @pl.loop(4, 8)
    def _(pos):
        correlate(pos)

        @pl.when(pos == 5)
        def _():
            ring_step(2)
    got(dxr.at[7], sdx.at[7], rdx.at[7])
    for sub in range(4):
        rows = pl.ds(128 * sub, 128)
        deliver(2, sub, dall[7, core, rows, :] + dxr[7, rows, :].astype(F32))
    for j in range(4):
        got(rrecv.at[pl.ds(32 * j, 32)], so.at[j], ro.at[j])
    res_ref[...] = rrecv[...].astype(F32).T.astype(BF)
    ring_step(3)
    for sub in range(4):
        cols = pl.ds(128 * sub, 128)
        for n in (2, 0, 1):
            for j in range(4):
                got(fr.at[n, pl.ds(32 * j, 32), cols], sf.at[n, sub, j], rf.at[n, sub, j])
        total = fr[0, :, cols].astype(F32) + fr[1, :, cols].astype(F32) + fr[2, :, cols].astype(F32)
        new_ref[:, cols] = par_ref[:, cols] + total * (0.5 / math.sqrt(24576))

    for wait in sent:
        wait()

    @pl.loop(0, 8)
    def _(pos):
        send(dxs.at[pos], dxr.at[pos], sdx.at[pos], rdx.at[pos], partner).wait_send()
    for way in range(2):
        for sub in range(4):
            for j in range(4):
                send(*delivery(way, sub, j)).wait_send()
    for step in range(3):
        for n, (way, subs) in enumerate(ways):
            if step or n < 2:
                for sub in subs:
                    send(gs.at[way, step, sub], gr.at[way, step, sub], sg.at[way, step, sub], rg.at[way, step, sub],
                         along(1 if way == 0 else -1)).wait_send()


def on_device(records, measured, markov_params, seg_lengths):
    dma = pltpu.SemaphoreType.DMA
    new, res = pl.pallas_call(
        body,
        out_shape=(jax.ShapeDtypeStruct((128, 512), F32), jax.ShapeDtypeStruct((384, 128), BF)),
        in_specs=[pl.BlockSpec(memory_space=pltpu.SMEM)] + [pl.BlockSpec(memory_space=pltpu.VMEM)] * 3,
        out_specs=(pl.BlockSpec(memory_space=pltpu.VMEM), pl.BlockSpec(memory_space=pltpu.VMEM)),
        scratch_shapes=[
            pltpu.VMEM((128, 512), BF),
            pltpu.VMEM((2048, 512), BF),
            pltpu.VMEM((HALO + SPAN, 512), BF),
            pltpu.VMEM((512, HALO + SPAN), BF),
            pltpu.VMEM((128, 384), BF),
            pltpu.VMEM((4, 32, 384), BF),
            pltpu.VMEM((128, SPAN), F32),
            pltpu.VMEM((SPAN, 128), F32),
            pltpu.VMEM((8, 128), F32),
            pltpu.VMEM((4, 8, 128), F32),
            pltpu.VMEM((1664, 256), F32),
            pltpu.VMEM((1552, 128), F32),
            pltpu.VMEM((1544, 128), F32),
            pltpu.VMEM((1744, 128), F32),
            pltpu.VMEM((1736, 128), F32),
            pltpu.VMEM((1732, 128), F32),
            pltpu.VMEM((2, 1712, 256), BF),
            pltpu.VMEM((4, 32, 384), BF),
            pltpu.VMEM((128, 384), BF),
            pltpu.VMEM((8, 2, 512, 128), F32),
            pltpu.VMEM((8, 512, 128), BF),
            pltpu.VMEM((8, 512, 128), BF),
            pltpu.VMEM((2, 3, 4, 128, 128), BF),
            pltpu.VMEM((2, 3, 4, 128, 128), BF),
            pltpu.VMEM((3, 128, 512), BF),
            pltpu.VMEM((3, 128, 512), BF),
            dma((4,)), dma((4,)), dma((4,)), dma((4, 3)), dma((2, 3)), dma((16,)), dma((4,)), dma((4,)), dma((4,)), dma((4,)),
            dma((4,)), dma((4,)), dma((1,)), dma((1,)),
            dma((2, 4, 4)), dma((2, 4, 4)), dma((8, 4)), dma((8, 4)),
            dma((8,)), dma((8,)), dma((2, 3, 4)), dma((2, 3, 4)), dma((3, 4, 4)), dma((3, 4, 4)),
        ],
        compiler_params=pltpu.CompilerParams(collective_id=0, has_side_effects=True, vmem_limit_bytes=56 * 1024 * 1024),
        name="gradient_step",
    )(seg_lengths, records, measured, markov_params.reshape(128, 512))
    return new.reshape(1, 128, 512), res


def solution(mesh):
    in_specs = (P("tm", "grp"), P("tm", "grp"), P("tm", "grp", None), P("tm"))
    out_specs = (P("tm", "grp", None), P("tm", "grp"))
    return jax.shard_map(on_device, mesh=mesh, in_specs=in_specs, out_specs=out_specs, check_vma=False)
```

```python
import math

import jax
import jax.numpy as jnp
from jax import lax
from jax.experimental import pallas as pl
from jax.experimental.pallas import tpu as pltpu
from jax.sharding import PartitionSpec as P

M = 512
LAGS = 64
BF = jnp.bfloat16
F32 = jnp.float32
HALO = 128
SPAN = 1536


def body(len_ref, rec_ref, meas_ref, par_ref, new_ref, res_ref, wsend, wbuf, xbuf, xt, msend, mrecv, mtf, mtime, lsend,
         lraw, acc, cbuf, ubuf, rp, wq, qq, qs, rsend, rrecv, dall, dxs, dxr, gs, gr, fs, fr,
         sb1, rb1, sa, sa2, sb2, ra, sm, rm, sl, rl, so, ro, sh, rh, sring, rring, spair, rpair, sdx, rdx, sg, rg, sf, rf):
    tm = lax.axis_index("tm")
    grp = lax.axis_index("grp")
    z = tm // 8
    yh = (tm // 4) % 2
    x = tm % 4
    yl = grp // 2
    core = grp % 2
    q = yl * 2 + yh
    home = yh == core

    def spread(j, dz=0):
        return lax.rem(z + dz + 8, 8) * 8 + core * 4 + j, yl * 2 + yh

    def along(step):
        return lax.rem(z + step + 8, 8) * 8 + yh * 4 + x, grp

    def over_x(k):
        return z * 8 + yh * 4 + lax.rem(x + k, 4), grp

    def over_y(k):
        j = lax.rem(q + k, 4)
        return z * 8 + (j % 2) * 4 + x, (j // 2) * 2 + core

    partner = (tm, yl * 2 + 1 - core)
    ahead = (lax.rem(z + core, 8) * 8 + yh * 4 + x, yl * 2 + 1 - core)
    behind = (lax.rem(z + core + 7, 8) * 8 + yh * 4 + x, yl * 2 + 1 - core)

    def first_hop(j):
        xj = core * x + (1 - core) * j
        yhj = core * (j % 2) + (1 - core) * yh
        ylj = core * (j // 2) + (1 - core) * yl
        return z * 8 + yhj * 4 + xj, ylj * 2 + yh

    def hop_from(j, c):
        if c == 0:
            return z * 8 + yh * 4 + j, yl * 2
        return z * 8 + core * 4 + x, j * 2 + 1

    def is_me(dev):
        return jnp.logical_and(dev[0] == tm, dev[1] == grp)

    def where(dev):
        return dict(device_id={"tm": dev[0], "grp": dev[1]}, device_id_type=pl.DeviceIdType.MESH)

    def send(src, dst, ssem, rsem, dev):
        return pltpu.make_async_remote_copy(src_ref=src, dst_ref=dst, send_sem=ssem, recv_sem=rsem, **where(dev))

    sent = []

    def go(src, dst, ssem, rsem, dev, only=None):
        if only is None:
            send(src, dst, ssem, rsem, dev).start()
            sent.append(lambda: send(src, dst, ssem, rsem, dev).wait_send())
            return

        @pl.when(only)
        def _():
            send(src, dst, ssem, rsem, dev).start()

        def wait():
            @pl.when(only)
            def _():
                send(src, dst, ssem, rsem, dev).wait_send()
        sent.append(wait)

    def go_any(src, dst, ssem, rsem, dev):
        me = is_me(dev)

        @pl.when(me)
        def _():
            pltpu.make_async_copy(src, dst, rsem).start()
        go(src, dst, ssem, rsem, dev, jnp.logical_not(me))

    def got(dst, ssem, rsem):
        send(dst, dst, ssem, rsem, partner).wait_recv()

    barrier = pltpu.get_barrier_semaphore()
    count = jnp.int32(0)
    friends = [(spread(j, dz), True) for dz in (1, -1) for j in range(4)] + [(spread(j), True) for j in range(4)] + [(first_hop(j), True) for j in range(4)]
    friends += [(hop_from(j, 0), home) for j in range(4)] + [(hop_from(j, 1), True) for j in range(2)]
    for n, (dev, holds) in enumerate(friends):
        other = jnp.logical_and(jnp.logical_not(is_me(dev)), holds)
        count = count + other.astype(jnp.int32)

        @pl.when(other)
        def _():
            pl.semaphore_signal(barrier, inc=1, **where(dev))
    sure = [over_x(k) for k in (1, 2, 3)] + [over_y(k) for k in (1, 2, 3)]
    sure += [along(1), along(-1), partner, ahead, behind]
    for dev in sure:
        pl.semaphore_signal(barrier, inc=1, **where(dev))
    wsend[...] = par_ref[...].astype(BF)
    lsend[...] = jnp.full((8, 128), len_ref[0], jnp.int32).astype(F32)
    pl.semaphore_wait(barrier, count + len(sure))

    def lag_rows(chunk, half, sub):
        return wbuf.at[pl.ds(pl.multiple_of(lax.rem(chunk + 8, 8) * 256 + half * 128 + sub * 32, 32), 32)]

    def slot(g, j):
        return xbuf.at[g, pl.ds(pl.multiple_of(HALO + 384 * j, 128), 384)]

    for j in range(4):
        go_any(wsend.at[pl.ds(32 * j, 32)], lag_rows(z, yh, x), sb1.at[j], rb1.at[x], spread(j))
    for j in range(4):
        go_any(rec_ref, slot(grp, x), sa.at[j], ra.at[grp * 4 + x], first_hop(j))

    msend[...] = meas_ref[...].astype(F32).T.astype(BF)
    for j in range(4):
        go_any(msend.at[pl.ds(32 * j, 32)], mrecv.at[x], sm.at[j], rm.at[x], spread(j))
        go_any(lsend, lraw.at[x], sl.at[j], rl.at[x], spread(j))
    xbuf[:, 0:64, :] = jnp.zeros((4, 64, 128), BF)
    mtf[32:128, :] = jnp.zeros((96, SPAN), F32)
    rp[...] = jnp.zeros_like(rp)
    acc[...] = jnp.zeros_like(acc)

    def ring_send(way, step, sub):
        ref = lag_rows(z - step if way == 0 else z + step, core, sub)
        go(ref, ref, sring.at[way, step, sub], rring.at[way, step, sub], along(1 if way == 0 else -1))

    def ring_got(way, step, sub):
        ref = lag_rows(z - step if way == 0 else z + step, core, sub)
        got(ref, sring.at[way, step - 1, sub], rring.at[way, step - 1, sub])

    def pair_copy(way, step, sub):
        ref = lag_rows(z - step if way == 0 else z + step, core, sub)
        n = number(way, step)
        return send(ref, ref, spair.at[n, sub], rpair.at[n, sub], partner)

    def pair_send(way, step, sub):
        pair_copy(way, step, sub).start()
        sent.append(lambda: pair_copy(way, step, sub).wait_send())

    def pair_got(n, chunk, sub):
        got(lag_rows(chunk, 1 - core, sub), spair.at[n, sub], rpair.at[n, sub])

    def number(way, step):
        return 2 * step - 1 + (way if step < 4 else 0) if step else 0

    for sub in range(4):
        got(lag_rows(z, core, sub), sb1.at[sub], rb1.at[sub])
        ring_send(0, 0, sub)
        if sub >= 2:
            ring_send(1, 0, sub)
        pair_send(0, 0, sub)
    for sub in range(2):
        ring_send(1, 0, sub)

    def slot_got(g, j):
        got(slot(g, j), sa.at[0], ra.at[g * 4 + j])

    def turned(g, j):
        cols = pl.ds(pl.multiple_of(HALO + 384 * j, 128), 384)
        rows = pl.ds(pl.multiple_of(128 * g, 128), 128)
        xt[rows, cols] = xbuf[g, cols, :].T

    for n in range(2):
        slot_got(2 * n + 1, x)
    for k in (2, 1, 3):
        for n in range(2):
            g = 2 * n + 1
            go(slot(g, x), slot(g, x), sb2.at[n, k - 1], ra.at[g * 4 + x], over_x(k))
    for n in range(4):
        j = lax.rem(x + 4 - n, 4)

        @pl.when(home)
        def _():
            slot_got(yl * 2, j)
        for k in (2, 1, 3):
            go(slot(yl * 2, j), slot(yl * 2, j), sa2.at[n, k - 1], ra.at[yl * 8 + j], over_y(k), home)

    def arrived(n):
        j = lax.rem(x + 4 - n, 4)

        @pl.when(jnp.logical_not(home))
        def _():
            slot_got(yl * 2, j)
        slot_got(2 * (1 - yl), j)
        for g in range(4):
            if n and g % 2:
                slot_got(g, j)
            turned(g, j)

    ways = ((0, (0, 1)), (1, (2, 3)), (0, (2, 3)), (1, (0, 1)))
    def passed_on(step):
        for n, (way, subs) in enumerate(ways):
            if step == 4 and n >= 2:
                continue
            for sub in subs:
                ring_got(way, step, sub)
                if step < 3 or (step == 3 and n < 2):
                    ring_send(way, step, sub)
                pair_send(way, step, sub)

    def paired(step):
        for n, (way, subs) in enumerate(ways):
            if step == 4 and n >= 2:
                continue
            for sub in subs:
                pair_got(number(way, step), z - step if way == 0 else z + step, sub)

    halo_rows = xbuf.at[:, pl.ds(HALO - 64, 64)]
    last_rows = xbuf.at[:, pl.ds(HALO + SPAN - 64, 64)]

    def forward(c, lo, rows):
        part = lax.dot_general(jnp.concatenate([xbuf[g, lo:lo + rows, :] for g in range(4)], 1), wbuf[pl.ds(pl.multiple_of(c * 256, 256), 256), :],
                               (((1,), (1,)), ((), ())), preferred_element_type=F32)
        acc[pl.ds(pl.multiple_of(lo - 64 + 8 * c, 8), rows), :] += part

    for step in range(1, 4):
        passed_on(step)
    for j in range(4):
        got(mrecv.at[j], sm.at[j], rm.at[j])
        got(lraw.at[j], sl.at[j], rl.at[j])
        mtf[0:32, 384 * j:384 * (j + 1)] = mrecv[j].astype(F32)
    mtime[...] = mtf[...].T
    for n in range(4):
        arrived(n)
    go(last_rows, halo_rows, sh.at[0], rh.at[0], ahead)
    for sub in range(4):
        pair_got(0, z, sub)
    for step in range(1, 4):
        paired(step)

    def chunk(i):
        return lax.rem(z + 8 + (1 - 2 * (i % 2)) * ((i + 1) // 2), 8)

    @pl.loop(0, 4)
    def _(i):
        forward(chunk(i), HALO, SPAN)
    got(halo_rows, sh.at[0], rh.at[0])
    first = jnp.logical_and(z == 0, core == 0)
    for g in range(4):
        halo = xbuf[g, HALO - 64:HALO, :]
        xbuf[g, HALO - 64:HALO, :] = jnp.where(first, jnp.zeros_like(halo), halo)
        xt[128 * g:128 * (g + 1), 0:HALO] = xbuf[g, 0:HALO, :].T

    @pl.loop(4, 8)
    def _(i):
        @pl.when(i == 5)
        def _():
            passed_on(4)

        @pl.when(i == 7)
        def _():
            paired(4)
        forward(chunk(i), HALO - 64, SPAN + 64)

    @pl.loop(0, 4)
    def _(i):
        forward(chunk(i), HALO - 64, 64)

    cbuf[...] = acc[48:1600, 0:128] + acc[44:1596, 128:256]
    ubuf[...] = cbuf[8:1552, :] + pltpu.roll(cbuf[6:1550, :], 64, 1)
    lane = lax.broadcasted_iota(jnp.int32, (384, 128), 1)
    row = lax.broadcasted_iota(jnp.int32, (384, 128), 0).astype(F32)
    for j in range(4):
        lo = 384 * j
        total = ubuf[lo + 8:lo + 392, :] + pltpu.roll(ubuf[lo + 7:lo + 391, :], 96, 1)
        gap = mtime[lo:lo + 384, :] - total * (1.0 / math.sqrt(LAGS * M))
        keep = jnp.logical_and(row < lraw[j, 0:1, :], lane < 32)
        rp[HALO + lo:HALO + lo + 384, :] = jnp.where(keep, gap, 0.0).astype(BF).astype(F32)
    wq[...] = rp[0:1736, :] + pltpu.roll(rp[1:1737, :], 32, 1)
    qq[...] = wq[0:1732, :] + pltpu.roll(wq[2:1734, :], 64, 1)
    for n in range(2):
        qs[n, :, 0:128] = qq[8 * n:8 * n + 1712, :].astype(BF)
        qs[n, :, 128:256] = qq[8 * n + 4:8 * n + 1716, :].astype(BF)

    def ring_add(step, way, sub):
        at = 2 * step - (1 if way == 0 and step > 0 else 0)
        rows = pl.ds(128 * sub, 128)
        own = dall[at, core, rows, :] + dxr[at, rows, :].astype(F32)
        early = (sub < 2) == (way == 0)
        if step > (0 if early else 1):
            got(gr.at[way, step - 1, sub], sg.at[way, step - 1, sub], rg.at[way, step - 1, sub])
            own = own + gr[way, step - 1, sub].astype(F32)
        if step == 3:
            deliver(way, sub, own)
            return
        gs[way, step, sub] = own.astype(BF)
        send(gs.at[way, step, sub], gr.at[way, step, sub], sg.at[way, step, sub], rg.at[way, step, sub],
             along(1 if way == 0 else -1)).start()

    def delivery(n, sub, j):
        return (fs.at[n, sub, pl.ds(32 * j, 32)], fr.at[n, sub, pl.ds(pl.multiple_of(32 * x, 32), 32)], sf.at[n, sub, j],
                rf.at[n, sub, x], spread(j, (1, -1, 0)[n]))

    def deliver(n, sub, part):
        fs[n, sub] = part.T.astype(BF)
        for j in range(4):
            if n < 2:
                send(*delivery(n, sub, j)).start()
            else:
                go_any(*delivery(n, sub, j))

    def correlate(pos):
        m = (pos + 1) // 2
        zc = lax.rem(z + 8 + (4 - m) * (2 * (pos % 2) - 1), 8)
        odd = zc % 2
        part = jnp.dot(xt[...], qs[odd, pl.ds(pl.multiple_of(8 * (zc - odd), 16), HALO + SPAN), :],
                       preferred_element_type=F32)
        dall[pos, 0] = part[:, 0:128]
        dall[pos, 1] = part[:, 128:256]
        dxs[pos] = dall[pos, 1 - core].astype(BF)
        send(dxs.at[pos], dxr.at[pos], sdx.at[pos], rdx.at[pos], partner).start()

    def ring_step(step):
        for at in ((2 * step - 1, 2 * step) if step else (0,)):
            got(dxr.at[at], sdx.at[at], rdx.at[at])
        for n in (2, 3, 0, 1) if step else (0, 1):
            way, subs = ways[n]
            for sub in subs:
                ring_add(step, way, sub)

    @pl.loop(0, 4)
    def _(pos):
        correlate(pos)
        for step in range(2):
            @pl.when(pos == 2 * step + 1)
            def _():
                ring_step(step)

    back = rp[HALO:HALO + SPAN, :].T
    for j in range(4):
        rsend[j] = back[0:32, 384 * j:384 * (j + 1)].astype(BF)
        go_any(rsend.at[j], rrecv.at[pl.ds(pl.multiple_of(32 * x, 32), 32)], so.at[j], ro.at[x], spread(j))

    @pl.loop(4, 8)
    def _(pos):
        correlate(pos)

        @pl.when(pos == 5)
        def _():
            ring_step(2)
    got(dxr.at[7], sdx.at[7], rdx.at[7])
    for sub in range(4):
        rows = pl.ds(128 * sub, 128)
        deliver(2, sub, dall[7, core, rows, :] + dxr[7, rows, :].astype(F32))
    for j in range(4):
        got(rrecv.at[pl.ds(32 * j, 32)], so.at[j], ro.at[j])
    res_ref[...] = rrecv[...].astype(F32).T.astype(BF)
    ring_step(3)
    for sub in range(4):
        cols = pl.ds(128 * sub, 128)
        for n in (2, 0, 1):
            for j in range(4):
                got(fr.at[n, sub, pl.ds(32 * j, 32)], sf.at[n, sub, j], rf.at[n, sub, j])
        total = fr[0, sub].astype(F32) + fr[1, sub].astype(F32) + fr[2, sub].astype(F32)
        new_ref[:, cols] = par_ref[:, cols] + total * (0.5 / math.sqrt(24576))

    for wait in sent:
        wait()

    @pl.loop(0, 8)
    def _(pos):
        send(dxs.at[pos], dxr.at[pos], sdx.at[pos], rdx.at[pos], partner).wait_send()
    for way in range(2):
        for sub in range(4):
            for j in range(4):
                send(*delivery(way, sub, j)).wait_send()
    for step in range(3):
        for n, (way, subs) in enumerate(ways):
            if step or n < 2:
                for sub in subs:
                    send(gs.at[way, step, sub], gr.at[way, step, sub], sg.at[way, step, sub], rg.at[way, step, sub],
                         along(1 if way == 0 else -1)).wait_send()


def on_device(records, measured, markov_params, seg_lengths):
    dma = pltpu.SemaphoreType.DMA
    new, res = pl.pallas_call(
        body,
        out_shape=(jax.ShapeDtypeStruct((128, 512), F32), jax.ShapeDtypeStruct((384, 128), BF)),
        in_specs=[pl.BlockSpec(memory_space=pltpu.SMEM)] + [pl.BlockSpec(memory_space=pltpu.VMEM)] * 3,
        out_specs=(pl.BlockSpec(memory_space=pltpu.VMEM), pl.BlockSpec(memory_space=pltpu.VMEM)),
        scratch_shapes=[
            pltpu.VMEM((128, 512), BF),
            pltpu.VMEM((2048, 512), BF),
            pltpu.VMEM((4, HALO + SPAN, 128), BF),
            pltpu.VMEM((512, HALO + SPAN), BF),
            pltpu.VMEM((128, 384), BF),
            pltpu.VMEM((4, 32, 384), BF),
            pltpu.VMEM((128, SPAN), F32),
            pltpu.VMEM((SPAN, 128), F32),
            pltpu.VMEM((8, 128), F32),
            pltpu.VMEM((4, 8, 128), F32),
            pltpu.VMEM((1664, 256), F32),
            pltpu.VMEM((1552, 128), F32),
            pltpu.VMEM((1544, 128), F32),
            pltpu.VMEM((1744, 128), F32),
            pltpu.VMEM((1736, 128), F32),
            pltpu.VMEM((1732, 128), F32),
            pltpu.VMEM((2, 1712, 256), BF),
            pltpu.VMEM((4, 32, 384), BF),
            pltpu.VMEM((128, 384), BF),
            pltpu.VMEM((8, 2, 512, 128), F32),
            pltpu.VMEM((8, 512, 128), BF),
            pltpu.VMEM((8, 512, 128), BF),
            pltpu.VMEM((2, 3, 4, 128, 128), BF),
            pltpu.VMEM((2, 3, 4, 128, 128), BF),
            pltpu.VMEM((3, 4, 128, 128), BF),
            pltpu.VMEM((3, 4, 128, 128), BF),
            dma((4,)), dma((4,)), dma((4,)), dma((4, 3)), dma((2, 3)), dma((16,)), dma((4,)), dma((4,)), dma((4,)), dma((4,)),
            dma((4,)), dma((4,)), dma((1,)), dma((1,)),
            dma((2, 4, 4)), dma((2, 4, 4)), dma((8, 4)), dma((8, 4)),
            dma((8,)), dma((8,)), dma((2, 3, 4)), dma((2, 3, 4)), dma((3, 4, 4)), dma((3, 4, 4)),
        ],
        compiler_params=pltpu.CompilerParams(collective_id=0, has_side_effects=True, vmem_limit_bytes=34 * 1024 * 1024),
        name="gradient_step",
    )(seg_lengths, records, measured, markov_params.reshape(128, 512))
    return new.reshape(1, 128, 512), res


def solution(mesh):
    in_specs = (P("tm", "grp"), P("tm", "grp"), P("tm", "grp", None), P("tm"))
    out_specs = (P("tm", "grp", None), P("tm", "grp"))
    return jax.shard_map(on_device, mesh=mesh, in_specs=in_specs, out_specs=out_specs, check_vma=False)
```

```python
import math

import jax
import jax.numpy as jnp
from jax import lax
from jax.experimental import pallas as pl
from jax.experimental.pallas import tpu as pltpu
from jax.sharding import PartitionSpec as P

M = 512
LAGS = 64
BF = jnp.bfloat16
F32 = jnp.float32
HALO = 128
SPAN = 1536


def body(len_ref, rec_ref, meas_hbm, par_hbm, new_ref, res_ref, meas_ref, par_ref, sin, wsend, wbuf, xbuf, xt, msend, mrecv, mtf, mtime, lsend,
         lraw, acc, cbuf, ubuf, rp, wq, qq, qs, rsend, rrecv, dall, dxs, dxr, gs, gr, fs, fr,
         sb1, rb1, sa, sa2, sb2, ra, sm, rm, sl, rl, so, ro, sh, rh, sring, rring, spair, rpair, sdx, rdx, sg, rg, sf, rf):
    tm = lax.axis_index("tm")
    grp = lax.axis_index("grp")
    z = tm // 8
    yh = (tm // 4) % 2
    x = tm % 4
    yl = grp // 2
    core = grp % 2
    q = yl * 2 + yh
    home = yh == core

    def spread(j, dz=0):
        return lax.rem(z + dz + 8, 8) * 8 + core * 4 + j, yl * 2 + yh

    def along(step):
        return lax.rem(z + step + 8, 8) * 8 + yh * 4 + x, grp

    def over_x(k):
        return z * 8 + yh * 4 + lax.rem(x + k, 4), grp

    def over_y(k):
        j = lax.rem(q + k, 4)
        return z * 8 + (j % 2) * 4 + x, (j // 2) * 2 + core

    partner = (tm, yl * 2 + 1 - core)
    ahead = (lax.rem(z + core, 8) * 8 + yh * 4 + x, yl * 2 + 1 - core)
    behind = (lax.rem(z + core + 7, 8) * 8 + yh * 4 + x, yl * 2 + 1 - core)

    def first_hop(j):
        xj = core * x + (1 - core) * j
        yhj = core * (j % 2) + (1 - core) * yh
        ylj = core * (j // 2) + (1 - core) * yl
        return z * 8 + yhj * 4 + xj, ylj * 2 + yh

    def hop_from(j, c):
        if c == 0:
            return z * 8 + yh * 4 + j, yl * 2
        return z * 8 + core * 4 + x, j * 2 + 1

    def is_me(dev):
        return jnp.logical_and(dev[0] == tm, dev[1] == grp)

    def where(dev):
        return dict(device_id={"tm": dev[0], "grp": dev[1]}, device_id_type=pl.DeviceIdType.MESH)

    def send(src, dst, ssem, rsem, dev):
        return pltpu.make_async_remote_copy(src_ref=src, dst_ref=dst, send_sem=ssem, recv_sem=rsem, **where(dev))

    sent = []

    def go(src, dst, ssem, rsem, dev, only=None):
        if only is None:
            send(src, dst, ssem, rsem, dev).start()
            sent.append(lambda: send(src, dst, ssem, rsem, dev).wait_send())
            return

        @pl.when(only)
        def _():
            send(src, dst, ssem, rsem, dev).start()

        def wait():
            @pl.when(only)
            def _():
                send(src, dst, ssem, rsem, dev).wait_send()
        sent.append(wait)

    def go_any(src, dst, ssem, rsem, dev):
        me = is_me(dev)

        @pl.when(me)
        def _():
            pltpu.make_async_copy(src, dst, rsem).start()
        go(src, dst, ssem, rsem, dev, jnp.logical_not(me))

    def got(dst, ssem, rsem):
        send(dst, dst, ssem, rsem, partner).wait_recv()

    loads = [pltpu.make_async_copy(par_hbm, par_ref, sin.at[0]), pltpu.make_async_copy(meas_hbm, meas_ref, sin.at[1])]
    for load in loads:
        load.start()

    barrier = pltpu.get_barrier_semaphore()
    count = jnp.int32(0)
    friends = [(spread(j, dz), True) for dz in (1, -1) for j in range(4)] + [(spread(j), True) for j in range(4)] + [(first_hop(j), True) for j in range(4)]
    friends += [(hop_from(j, 0), home) for j in range(4)] + [(hop_from(j, 1), True) for j in range(2)]
    for n, (dev, holds) in enumerate(friends):
        other = jnp.logical_and(jnp.logical_not(is_me(dev)), holds)
        count = count + other.astype(jnp.int32)

        @pl.when(other)
        def _():
            pl.semaphore_signal(barrier, inc=1, **where(dev))
    sure = [over_x(k) for k in (1, 2, 3)] + [over_y(k) for k in (1, 2, 3)]
    sure += [along(1), along(-1), partner, ahead, behind]
    for dev in sure:
        pl.semaphore_signal(barrier, inc=1, **where(dev))
    loads[0].wait()
    wsend[...] = par_ref[...].astype(BF)
    lsend[...] = jnp.full((8, 128), len_ref[0], jnp.int32).astype(F32)
    pl.semaphore_wait(barrier, count + len(sure))

    def lag_rows(chunk, half, sub):
        return wbuf.at[pl.ds(pl.multiple_of(lax.rem(chunk + 8, 8) * 256 + half * 128 + sub * 32, 32), 32)]

    def slot(g, j):
        return xbuf.at[g, pl.ds(pl.multiple_of(HALO + 384 * j, 128), 384)]

    for j in range(4):
        go_any(wsend.at[pl.ds(32 * j, 32)], lag_rows(z, yh, x), sb1.at[j], rb1.at[x], spread(j))
    for j in range(4):
        go_any(rec_ref, slot(grp, x), sa.at[j], ra.at[grp * 4 + x], first_hop(j))

    loads[1].wait()
    msend[...] = meas_ref[...].astype(F32).T.astype(BF)
    for j in range(4):
        go_any(msend.at[pl.ds(32 * j, 32)], mrecv.at[x], sm.at[j], rm.at[x], spread(j))
        go_any(lsend, lraw.at[x], sl.at[j], rl.at[x], spread(j))
    xbuf[:, 0:64, :] = jnp.zeros((4, 64, 128), BF)
    mtf[32:128, :] = jnp.zeros((96, SPAN), F32)
    rp[...] = jnp.zeros_like(rp)
    acc[...] = jnp.zeros_like(acc)

    def ring_send(way, step, sub):
        ref = lag_rows(z - step if way == 0 else z + step, core, sub)
        go(ref, ref, sring.at[way, step, sub], rring.at[way, step, sub], along(1 if way == 0 else -1))

    def ring_got(way, step, sub):
        ref = lag_rows(z - step if way == 0 else z + step, core, sub)
        got(ref, sring.at[way, step - 1, sub], rring.at[way, step - 1, sub])

    def pair_copy(way, step, sub):
        ref = lag_rows(z - step if way == 0 else z + step, core, sub)
        n = number(way, step)
        return send(ref, ref, spair.at[n, sub], rpair.at[n, sub], partner)

    def pair_send(way, step, sub):
        pair_copy(way, step, sub).start()
        sent.append(lambda: pair_copy(way, step, sub).wait_send())

    def pair_got(n, chunk, sub):
        got(lag_rows(chunk, 1 - core, sub), spair.at[n, sub], rpair.at[n, sub])

    def number(way, step):
        return 2 * step - 1 + (way if step < 4 else 0) if step else 0

    for sub in range(4):
        got(lag_rows(z, core, sub), sb1.at[sub], rb1.at[sub])
        ring_send(0, 0, sub)
        if sub >= 2:
            ring_send(1, 0, sub)
        pair_send(0, 0, sub)
    for sub in range(2):
        ring_send(1, 0, sub)

    def slot_got(g, j):
        got(slot(g, j), sa.at[0], ra.at[g * 4 + j])

    def turned(g, j):
        cols = pl.ds(pl.multiple_of(HALO + 384 * j, 128), 384)
        rows = pl.ds(pl.multiple_of(128 * g, 128), 128)
        xt[rows, cols] = xbuf[g, cols, :].T

    for n in range(2):
        slot_got(2 * n + 1, x)
    for k in (2, 1, 3):
        for n in range(2):
            g = 2 * n + 1
            go(slot(g, x), slot(g, x), sb2.at[n, k - 1], ra.at[g * 4 + x], over_x(k))
    for n in range(4):
        j = lax.rem(x + 4 - n, 4)

        @pl.when(home)
        def _():
            slot_got(yl * 2, j)
        for k in (2, 1, 3):
            go(slot(yl * 2, j), slot(yl * 2, j), sa2.at[n, k - 1], ra.at[yl * 8 + j], over_y(k), home)

    def arrived(n):
        j = lax.rem(x + 4 - n, 4)

        @pl.when(jnp.logical_not(home))
        def _():
            slot_got(yl * 2, j)
        slot_got(2 * (1 - yl), j)
        for g in range(4):
            if n and g % 2:
                slot_got(g, j)
            turned(g, j)

    ways = ((0, (0, 1)), (1, (2, 3)), (0, (2, 3)), (1, (0, 1)))
    def passed_on(step):
        for n, (way, subs) in enumerate(ways):
            if step == 4 and n >= 2:
                continue
            for sub in subs:
                ring_got(way, step, sub)
                if step < 3 or (step == 3 and n < 2):
                    ring_send(way, step, sub)
                pair_send(way, step, sub)

    def paired(step):
        for n, (way, subs) in enumerate(ways):
            if step == 4 and n >= 2:
                continue
            for sub in subs:
                pair_got(number(way, step), z - step if way == 0 else z + step, sub)

    halo_rows = xbuf.at[:, pl.ds(HALO - 64, 64)]
    last_rows = xbuf.at[:, pl.ds(HALO + SPAN - 64, 64)]

    def forward(c, lo, rows):
        part = lax.dot_general(jnp.concatenate([xbuf[g, lo:lo + rows, :] for g in range(4)], 1), wbuf[pl.ds(pl.multiple_of(c * 256, 256), 256), :],
                               (((1,), (1,)), ((), ())), preferred_element_type=F32)
        acc[pl.ds(pl.multiple_of(lo - 64 + 8 * c, 8), rows), :] += part

    for step in range(1, 4):
        passed_on(step)
    for j in range(4):
        got(mrecv.at[j], sm.at[j], rm.at[j])
        got(lraw.at[j], sl.at[j], rl.at[j])
        mtf[0:32, 384 * j:384 * (j + 1)] = mrecv[j].astype(F32)
    mtime[...] = mtf[...].T
    for n in range(4):
        arrived(n)
    go(last_rows, halo_rows, sh.at[0], rh.at[0], ahead)
    for sub in range(4):
        pair_got(0, z, sub)
    for step in range(1, 4):
        paired(step)

    def chunk(i):
        return lax.rem(z + 8 + (1 - 2 * (i % 2)) * ((i + 1) // 2), 8)

    @pl.loop(0, 4)
    def _(i):
        forward(chunk(i), HALO, SPAN)
    got(halo_rows, sh.at[0], rh.at[0])
    first = jnp.logical_and(z == 0, core == 0)
    for g in range(4):
        halo = xbuf[g, HALO - 64:HALO, :]
        xbuf[g, HALO - 64:HALO, :] = jnp.where(first, jnp.zeros_like(halo), halo)
        xt[128 * g:128 * (g + 1), 0:HALO] = xbuf[g, 0:HALO, :].T

    @pl.loop(4, 8)
    def _(i):
        @pl.when(i == 5)
        def _():
            passed_on(4)

        @pl.when(i == 7)
        def _():
            paired(4)
        forward(chunk(i), HALO - 64, SPAN + 64)

    @pl.loop(0, 4)
    def _(i):
        forward(chunk(i), HALO - 64, 64)

    cbuf[...] = acc[48:1600, 0:128] + acc[44:1596, 128:256]
    ubuf[...] = cbuf[8:1552, :] + pltpu.roll(cbuf[6:1550, :], 64, 1)
    lane = lax.broadcasted_iota(jnp.int32, (384, 128), 1)
    row = lax.broadcasted_iota(jnp.int32, (384, 128), 0).astype(F32)
    for j in range(4):
        lo = 384 * j
        total = ubuf[lo + 8:lo + 392, :] + pltpu.roll(ubuf[lo + 7:lo + 391, :], 96, 1)
        gap = mtime[lo:lo + 384, :] - total * (1.0 / math.sqrt(LAGS * M))
        keep = jnp.logical_and(row < lraw[j, 0:1, :], lane < 32)
        rp[HALO + lo:HALO + lo + 384, :] = jnp.where(keep, gap, 0.0).astype(BF).astype(F32)
    wq[...] = rp[0:1736, :] + pltpu.roll(rp[1:1737, :], 32, 1)
    qq[...] = wq[0:1732, :] + pltpu.roll(wq[2:1734, :], 64, 1)
    for n in range(2):
        qs[n, :, 0:128] = qq[8 * n:8 * n + 1712, :].astype(BF)
        qs[n, :, 128:256] = qq[8 * n + 4:8 * n + 1716, :].astype(BF)

    def ring_add(step, way, sub):
        at = 2 * step - (1 if way == 0 and step > 0 else 0)
        rows = pl.ds(128 * sub, 128)
        own = dall[at, core, rows, :] + dxr[at, rows, :].astype(F32)
        early = (sub < 2) == (way == 0)
        if step > (0 if early else 1):
            got(gr.at[way, step - 1, sub], sg.at[way, step - 1, sub], rg.at[way, step - 1, sub])
            own = own + gr[way, step - 1, sub].astype(F32)
        if step == 3:
            deliver(way, sub, own)
            return
        gs[way, step, sub] = own.astype(BF)
        send(gs.at[way, step, sub], gr.at[way, step, sub], sg.at[way, step, sub], rg.at[way, step, sub],
             along(1 if way == 0 else -1)).start()

    def delivery(n, sub, j):
        return (fs.at[n, sub, pl.ds(32 * j, 32)], fr.at[n, sub, pl.ds(pl.multiple_of(32 * x, 32), 32)], sf.at[n, sub, j],
                rf.at[n, sub, x], spread(j, (1, -1, 0)[n]))

    def deliver(n, sub, part):
        fs[n, sub] = part.T.astype(BF)
        for j in range(4):
            if n < 2:
                send(*delivery(n, sub, j)).start()
            else:
                go_any(*delivery(n, sub, j))

    def correlate(pos):
        m = (pos + 1) // 2
        zc = lax.rem(z + 8 + (4 - m) * (2 * (pos % 2) - 1), 8)
        odd = zc % 2
        part = jnp.dot(xt[...], qs[odd, pl.ds(pl.multiple_of(8 * (zc - odd), 16), HALO + SPAN), :],
                       preferred_element_type=F32)
        dall[pos, 0] = part[:, 0:128]
        dall[pos, 1] = part[:, 128:256]
        dxs[pos] = dall[pos, 1 - core].astype(BF)
        send(dxs.at[pos], dxr.at[pos], sdx.at[pos], rdx.at[pos], partner).start()

    def ring_step(step):
        for at in ((2 * step - 1, 2 * step) if step else (0,)):
            got(dxr.at[at], sdx.at[at], rdx.at[at])
        for n in (2, 3, 0, 1) if step else (0, 1):
            way, subs = ways[n]
            for sub in subs:
                ring_add(step, way, sub)

    @pl.loop(0, 4)
    def _(pos):
        correlate(pos)
        for step in range(2):
            @pl.when(pos == 2 * step + 1)
            def _():
                ring_step(step)

    back = rp[HALO:HALO + SPAN, :].T
    for j in range(4):
        rsend[j] = back[0:32, 384 * j:384 * (j + 1)].astype(BF)
        go_any(rsend.at[j], rrecv.at[pl.ds(pl.multiple_of(32 * x, 32), 32)], so.at[j], ro.at[x], spread(j))

    @pl.loop(4, 8)
    def _(pos):
        correlate(pos)

        @pl.when(pos == 5)
        def _():
            ring_step(2)
    got(dxr.at[7], sdx.at[7], rdx.at[7])
    for sub in range(4):
        rows = pl.ds(128 * sub, 128)
        deliver(2, sub, dall[7, core, rows, :] + dxr[7, rows, :].astype(F32))
    for j in range(4):
        got(rrecv.at[pl.ds(32 * j, 32)], so.at[j], ro.at[j])
    res_ref[...] = rrecv[...].astype(F32).T.astype(BF)
    ring_step(3)
    for sub in range(4):
        cols = pl.ds(128 * sub, 128)
        for n in (2, 0, 1):
            for j in range(4):
                got(fr.at[n, sub, pl.ds(32 * j, 32)], sf.at[n, sub, j], rf.at[n, sub, j])
        total = fr[0, sub].astype(F32) + fr[1, sub].astype(F32) + fr[2, sub].astype(F32)
        new_ref[:, cols] = par_ref[:, cols] + total * (0.5 / math.sqrt(24576))

    for wait in sent:
        wait()

    @pl.loop(0, 8)
    def _(pos):
        send(dxs.at[pos], dxr.at[pos], sdx.at[pos], rdx.at[pos], partner).wait_send()
    for way in range(2):
        for sub in range(4):
            for j in range(4):
                send(*delivery(way, sub, j)).wait_send()
    for step in range(3):
        for n, (way, subs) in enumerate(ways):
            if step or n < 2:
                for sub in subs:
                    send(gs.at[way, step, sub], gr.at[way, step, sub], sg.at[way, step, sub], rg.at[way, step, sub],
                         along(1 if way == 0 else -1)).wait_send()


def on_device(records, measured, markov_params, seg_lengths):
    dma = pltpu.SemaphoreType.DMA
    new, res = pl.pallas_call(
        body,
        out_shape=(jax.ShapeDtypeStruct((128, 512), F32), jax.ShapeDtypeStruct((384, 128), BF)),
        in_specs=[pl.BlockSpec(memory_space=pltpu.SMEM)] + [pl.BlockSpec(memory_space=pltpu.HBM)] * 3,
        out_specs=(pl.BlockSpec(memory_space=pltpu.VMEM), pl.BlockSpec(memory_space=pltpu.VMEM)),
        scratch_shapes=[
            pltpu.VMEM((384, 128), BF),
            pltpu.VMEM((128, 512), F32),
            dma((2,)),
            pltpu.VMEM((128, 512), BF),
            pltpu.VMEM((2048, 512), BF),
            pltpu.VMEM((4, HALO + SPAN, 128), BF),
            pltpu.VMEM((512, HALO + SPAN), BF),
            pltpu.VMEM((128, 384), BF),
            pltpu.VMEM((4, 32, 384), BF),
            pltpu.VMEM((128, SPAN), F32),
            pltpu.VMEM((SPAN, 128), F32),
            pltpu.VMEM((8, 128), F32),
            pltpu.VMEM((4, 8, 128), F32),
            pltpu.VMEM((1664, 256), F32),
            pltpu.VMEM((1552, 128), F32),
            pltpu.VMEM((1544, 128), F32),
            pltpu.VMEM((1744, 128), F32),
            pltpu.VMEM((1736, 128), F32),
            pltpu.VMEM((1732, 128), F32),
            pltpu.VMEM((2, 1712, 256), BF),
            pltpu.VMEM((4, 32, 384), BF),
            pltpu.VMEM((128, 384), BF),
            pltpu.VMEM((8, 2, 512, 128), F32),
            pltpu.VMEM((8, 512, 128), BF),
            pltpu.VMEM((8, 512, 128), BF),
            pltpu.VMEM((2, 3, 4, 128, 128), BF),
            pltpu.VMEM((2, 3, 4, 128, 128), BF),
            pltpu.VMEM((3, 4, 128, 128), BF),
            pltpu.VMEM((3, 4, 128, 128), BF),
            dma((4,)), dma((4,)), dma((4,)), dma((4, 3)), dma((2, 3)), dma((16,)), dma((4,)), dma((4,)), dma((4,)), dma((4,)),
            dma((4,)), dma((4,)), dma((1,)), dma((1,)),
            dma((2, 4, 4)), dma((2, 4, 4)), dma((8, 4)), dma((8, 4)),
            dma((8,)), dma((8,)), dma((2, 3, 4)), dma((2, 3, 4)), dma((3, 4, 4)), dma((3, 4, 4)),
        ],
        compiler_params=pltpu.CompilerParams(collective_id=0, has_side_effects=True, vmem_limit_bytes=34 * 1024 * 1024),
        name="gradient_step",
    )(seg_lengths, *(pltpu.with_memory_space_constraint(a, pltpu.HBM) for a in (records, measured, markov_params.reshape(128, 512))))
    return new.reshape(1, 128, 512), res


def solution(mesh):
    in_specs = (P("tm", "grp"), P("tm", "grp"), P("tm", "grp", None), P("tm"))
    out_specs = (P("tm", "grp", None), P("tm", "grp"))
    return jax.shard_map(on_device, mesh=mesh, in_specs=in_specs, out_specs=out_specs, check_vma=False)
```

```python
import math

import jax
import jax.numpy as jnp
from jax import lax
from jax.experimental import pallas as pl
from jax.experimental.pallas import tpu as pltpu
from jax.sharding import PartitionSpec as P

M = 512
LAGS = 64
BF = jnp.bfloat16
F32 = jnp.float32
HALO = 128
SPAN = 1536


def body(len_ref, rec_ref, meas_hbm, par_hbm, new_ref, res_ref, meas_ref, par_ref, sin, wsend, wbuf, xbuf, xt, msend, mrecv, mtf, mtime, lsend,
         lraw, acc, cbuf, ubuf, rp, wq, qq, qs, rsend, rrecv, dall, dxs, dxr, gs, gr, fs, fr,
         sb1, rb1, sa, sa2, sb2, ra, sm, rm, sl, rl, so, ro, sh, rh, sring, rring, spair, rpair, sdx, rdx, sg, rg, sf, rf):
    tm = lax.axis_index("tm")
    grp = lax.axis_index("grp")
    z = tm // 8
    yh = (tm // 4) % 2
    x = tm % 4
    yl = grp // 2
    core = grp % 2
    q = yl * 2 + yh
    home = yh == core

    def spread(j, dz=0):
        return lax.rem(z + dz + 8, 8) * 8 + core * 4 + j, yl * 2 + yh

    def along(step):
        return lax.rem(z + step + 8, 8) * 8 + yh * 4 + x, grp

    def over_x(k):
        return z * 8 + yh * 4 + lax.rem(x + k, 4), grp

    def over_y(k):
        j = lax.rem(q + k, 4)
        return z * 8 + (j % 2) * 4 + x, (j // 2) * 2 + core

    partner = (tm, yl * 2 + 1 - core)
    ahead = (lax.rem(z + core, 8) * 8 + yh * 4 + x, yl * 2 + 1 - core)
    behind = (lax.rem(z + core + 7, 8) * 8 + yh * 4 + x, yl * 2 + 1 - core)

    def first_hop(j):
        xj = core * x + (1 - core) * j
        yhj = core * (j % 2) + (1 - core) * yh
        ylj = core * (j // 2) + (1 - core) * yl
        return z * 8 + yhj * 4 + xj, ylj * 2 + yh

    def hop_from(j, c):
        if c == 0:
            return z * 8 + yh * 4 + j, yl * 2
        return z * 8 + core * 4 + x, j * 2 + 1

    def is_me(dev):
        return jnp.logical_and(dev[0] == tm, dev[1] == grp)

    def where(dev):
        return dict(device_id={"tm": dev[0], "grp": dev[1]}, device_id_type=pl.DeviceIdType.MESH)

    def send(src, dst, ssem, rsem, dev):
        return pltpu.make_async_remote_copy(src_ref=src, dst_ref=dst, send_sem=ssem, recv_sem=rsem, **where(dev))

    sent = []

    def go(src, dst, ssem, rsem, dev, only=None):
        if only is None:
            send(src, dst, ssem, rsem, dev).start()
            sent.append(lambda: send(src, dst, ssem, rsem, dev).wait_send())
            return

        @pl.when(only)
        def _():
            send(src, dst, ssem, rsem, dev).start()

        def wait():
            @pl.when(only)
            def _():
                send(src, dst, ssem, rsem, dev).wait_send()
        sent.append(wait)

    def go_any(src, dst, ssem, rsem, dev):
        me = is_me(dev)

        @pl.when(me)
        def _():
            pltpu.make_async_copy(src, dst, rsem).start()
        go(src, dst, ssem, rsem, dev, jnp.logical_not(me))

    def got(dst, ssem, rsem):
        send(dst, dst, ssem, rsem, partner).wait_recv()

    loads = [pltpu.make_async_copy(par_hbm, par_ref, sin.at[0]), pltpu.make_async_copy(meas_hbm, meas_ref, sin.at[1])]
    for load in loads:
        load.start()

    barrier = pltpu.get_barrier_semaphore()
    count = jnp.int32(0)
    friends = [(spread(j, dz), True) for dz in (1, -1) for j in range(4)] + [(spread(j), True) for j in range(4)] + [(first_hop(j), True) for j in range(4)]
    friends += [(hop_from(j, 0), home) for j in range(4)] + [(hop_from(j, 1), True) for j in range(2)]
    for n, (dev, holds) in enumerate(friends):
        other = jnp.logical_and(jnp.logical_not(is_me(dev)), holds)
        count = count + other.astype(jnp.int32)

        @pl.when(other)
        def _():
            pl.semaphore_signal(barrier, inc=1, **where(dev))
    sure = [over_x(k) for k in (1, 2, 3)] + [over_y(k) for k in (1, 2, 3)]
    sure += [along(1), along(-1), partner, ahead, behind]
    for dev in sure:
        pl.semaphore_signal(barrier, inc=1, **where(dev))
    loads[0].wait()
    wsend[...] = par_ref[...].astype(BF)
    lsend[...] = jnp.full((8, 128), len_ref[0], jnp.int32).astype(F32)
    pl.semaphore_wait(barrier, count + len(sure))

    def lag_rows(chunk, half, sub):
        return wbuf.at[pl.ds(pl.multiple_of(lax.rem(chunk + 8, 8) * 256 + half * 128 + sub * 32, 32), 32)]

    def slot(g, j):
        return xbuf.at[g, pl.ds(pl.multiple_of(HALO + 384 * j, 128), 384)]

    for j in range(4):
        go_any(wsend.at[pl.ds(32 * j, 32)], lag_rows(z, yh, x), sb1.at[j], rb1.at[x], spread(j))
    for j in range(4):
        go_any(rec_ref, slot(grp, x), sa.at[j], ra.at[grp * 4 + x], first_hop(j))

    loads[1].wait()
    msend[...] = meas_ref[...].astype(F32).T.astype(BF)
    xbuf[:, 0:64, :] = jnp.zeros((4, 64, 128), BF)
    mtf[32:128, :] = jnp.zeros((96, SPAN), F32)
    rp[...] = jnp.zeros_like(rp)
    acc[...] = jnp.zeros_like(acc)

    def ring_send(way, step, sub):
        ref = lag_rows(z - step if way == 0 else z + step, core, sub)
        go(ref, ref, sring.at[way, step, sub], rring.at[way, step, sub], along(1 if way == 0 else -1))

    def ring_got(way, step, sub):
        ref = lag_rows(z - step if way == 0 else z + step, core, sub)
        got(ref, sring.at[way, step - 1, sub], rring.at[way, step - 1, sub])

    def pair_copy(way, step, sub):
        ref = lag_rows(z - step if way == 0 else z + step, core, sub)
        n = number(way, step)
        return send(ref, ref, spair.at[n, sub], rpair.at[n, sub], partner)

    def pair_send(way, step, sub):
        pair_copy(way, step, sub).start()
        sent.append(lambda: pair_copy(way, step, sub).wait_send())

    def pair_got(n, chunk, sub):
        got(lag_rows(chunk, 1 - core, sub), spair.at[n, sub], rpair.at[n, sub])

    def number(way, step):
        return 2 * step - 1 + (way if step < 4 else 0) if step else 0

    for sub in range(4):
        got(lag_rows(z, core, sub), sb1.at[sub], rb1.at[sub])
        ring_send(0, 0, sub)
        if sub >= 2:
            ring_send(1, 0, sub)
        pair_send(0, 0, sub)
    for sub in range(2):
        ring_send(1, 0, sub)

    def slot_got(g, j):
        got(slot(g, j), sa.at[0], ra.at[g * 4 + j])

    def turned(g, j):
        cols = pl.ds(pl.multiple_of(HALO + 384 * j, 128), 384)
        rows = pl.ds(pl.multiple_of(128 * g, 128), 128)
        xt[rows, cols] = xbuf[g, cols, :].T

    for n in range(2):
        slot_got(2 * n + 1, x)
    for k in (2, 1, 3):
        for n in range(2):
            g = 2 * n + 1
            go(slot(g, x), slot(g, x), sb2.at[n, k - 1], ra.at[g * 4 + x], over_x(k))
    for n in range(4):
        j = lax.rem(x + 4 - n, 4)

        @pl.when(home)
        def _():
            slot_got(yl * 2, j)
        for k in (2, 1, 3):
            go(slot(yl * 2, j), slot(yl * 2, j), sa2.at[n, k - 1], ra.at[yl * 8 + j], over_y(k), home)

    for j in range(4):
        go_any(msend.at[pl.ds(32 * j, 32)], mrecv.at[x], sm.at[j], rm.at[x], spread(j))
        go_any(lsend, lraw.at[x], sl.at[j], rl.at[x], spread(j))

    def arrived(n):
        j = lax.rem(x + 4 - n, 4)

        @pl.when(jnp.logical_not(home))
        def _():
            slot_got(yl * 2, j)
        slot_got(2 * (1 - yl), j)
        for g in range(4):
            if n and g % 2:
                slot_got(g, j)
            turned(g, j)

    ways = ((0, (0, 1)), (1, (2, 3)), (0, (2, 3)), (1, (0, 1)))
    def passed_on(step):
        for n, (way, subs) in enumerate(ways):
            if step == 4 and n >= 2:
                continue
            for sub in subs:
                ring_got(way, step, sub)
                if step < 3 or (step == 3 and n < 2):
                    ring_send(way, step, sub)
                pair_send(way, step, sub)

    def paired(step):
        for n, (way, subs) in enumerate(ways):
            if step == 4 and n >= 2:
                continue
            for sub in subs:
                pair_got(number(way, step), z - step if way == 0 else z + step, sub)

    halo_rows = xbuf.at[:, pl.ds(HALO - 64, 64)]
    last_rows = xbuf.at[:, pl.ds(HALO + SPAN - 64, 64)]

    def forward(c, lo, rows):
        part = lax.dot_general(jnp.concatenate([xbuf[g, lo:lo + rows, :] for g in range(4)], 1), wbuf[pl.ds(pl.multiple_of(c * 256, 256), 256), :],
                               (((1,), (1,)), ((), ())), preferred_element_type=F32)
        acc[pl.ds(pl.multiple_of(lo - 64 + 8 * c, 8), rows), :] += part

    for step in range(1, 4):
        passed_on(step)
    for n in range(4):
        arrived(n)
    go(last_rows, halo_rows, sh.at[0], rh.at[0], ahead)
    for sub in range(4):
        pair_got(0, z, sub)
    for step in range(1, 4):
        paired(step)

    def chunk(i):
        return lax.rem(z + 8 + (1 - 2 * (i % 2)) * ((i + 1) // 2), 8)

    @pl.loop(0, 4)
    def _(i):
        forward(chunk(i), HALO, SPAN)
    for j in range(4):
        got(mrecv.at[j], sm.at[j], rm.at[j])
        got(lraw.at[j], sl.at[j], rl.at[j])
        mtf[0:32, 384 * j:384 * (j + 1)] = mrecv[j].astype(F32)
    mtime[...] = mtf[...].T
    got(halo_rows, sh.at[0], rh.at[0])
    first = jnp.logical_and(z == 0, core == 0)
    for g in range(4):
        halo = xbuf[g, HALO - 64:HALO, :]
        xbuf[g, HALO - 64:HALO, :] = jnp.where(first, jnp.zeros_like(halo), halo)
        xt[128 * g:128 * (g + 1), 0:HALO] = xbuf[g, 0:HALO, :].T

    @pl.loop(4, 8)
    def _(i):
        @pl.when(i == 5)
        def _():
            passed_on(4)

        @pl.when(i == 7)
        def _():
            paired(4)
        forward(chunk(i), HALO - 64, SPAN + 64)

    @pl.loop(0, 4)
    def _(i):
        forward(chunk(i), HALO - 64, 64)

    cbuf[...] = acc[48:1600, 0:128] + acc[44:1596, 128:256]
    ubuf[...] = cbuf[8:1552, :] + pltpu.roll(cbuf[6:1550, :], 64, 1)
    lane = lax.broadcasted_iota(jnp.int32, (384, 128), 1)
    row = lax.broadcasted_iota(jnp.int32, (384, 128), 0).astype(F32)
    for j in range(4):
        lo = 384 * j
        total = ubuf[lo + 8:lo + 392, :] + pltpu.roll(ubuf[lo + 7:lo + 391, :], 96, 1)
        gap = mtime[lo:lo + 384, :] - total * (1.0 / math.sqrt(LAGS * M))
        keep = jnp.logical_and(row < lraw[j, 0:1, :], lane < 32)
        rp[HALO + lo:HALO + lo + 384, :] = jnp.where(keep, gap, 0.0).astype(BF).astype(F32)
    wq[...] = rp[0:1736, :] + pltpu.roll(rp[1:1737, :], 32, 1)
    qq[...] = wq[0:1732, :] + pltpu.roll(wq[2:1734, :], 64, 1)
    for n in range(2):
        qs[n, :, 0:128] = qq[8 * n:8 * n + 1712, :].astype(BF)
        qs[n, :, 128:256] = qq[8 * n + 4:8 * n + 1716, :].astype(BF)

    def ring_add(step, way, sub):
        at = 2 * step - (1 if way == 0 and step > 0 else 0)
        rows = pl.ds(128 * sub, 128)
        own = dall[at, core, rows, :] + dxr[at, rows, :].astype(F32)
        early = (sub < 2) == (way == 0)
        if step > (0 if early else 1):
            got(gr.at[way, step - 1, sub], sg.at[way, step - 1, sub], rg.at[way, step - 1, sub])
            own = own + gr[way, step - 1, sub].astype(F32)
        if step == 3:
            deliver(way, sub, own)
            return
        gs[way, step, sub] = own.astype(BF)
        send(gs.at[way, step, sub], gr.at[way, step, sub], sg.at[way, step, sub], rg.at[way, step, sub],
             along(1 if way == 0 else -1)).start()

    def delivery(n, sub, j):
        return (fs.at[n, sub, pl.ds(32 * j, 32)], fr.at[n, sub, pl.ds(pl.multiple_of(32 * x, 32), 32)], sf.at[n, sub, j],
                rf.at[n, sub, x], spread(j, (1, -1, 0)[n]))

    def deliver(n, sub, part):
        fs[n, sub] = part.T.astype(BF)
        for j in range(4):
            if n < 2:
                send(*delivery(n, sub, j)).start()
            else:
                go_any(*delivery(n, sub, j))

    def correlate(pos):
        m = (pos + 1) // 2
        zc = lax.rem(z + 8 + (4 - m) * (2 * (pos % 2) - 1), 8)
        odd = zc % 2
        part = jnp.dot(xt[...], qs[odd, pl.ds(pl.multiple_of(8 * (zc - odd), 16), HALO + SPAN), :],
                       preferred_element_type=F32)
        dall[pos, 0] = part[:, 0:128]
        dall[pos, 1] = part[:, 128:256]
        dxs[pos] = dall[pos, 1 - core].astype(BF)
        send(dxs.at[pos], dxr.at[pos], sdx.at[pos], rdx.at[pos], partner).start()

    def ring_step(step):
        for at in ((2 * step - 1, 2 * step) if step else (0,)):
            got(dxr.at[at], sdx.at[at], rdx.at[at])
        for n in (2, 3, 0, 1) if step else (0, 1):
            way, subs = ways[n]
            for sub in subs:
                ring_add(step, way, sub)

    @pl.loop(0, 4)
    def _(pos):
        correlate(pos)
        for step in range(2):
            @pl.when(pos == 2 * step + 1)
            def _():
                ring_step(step)

    back = rp[HALO:HALO + SPAN, :].T
    for j in range(4):
        rsend[j] = back[0:32, 384 * j:384 * (j + 1)].astype(BF)
        go_any(rsend.at[j], rrecv.at[pl.ds(pl.multiple_of(32 * x, 32), 32)], so.at[j], ro.at[x], spread(j))

    @pl.loop(4, 8)
    def _(pos):
        correlate(pos)

        @pl.when(pos == 5)
        def _():
            ring_step(2)
    got(dxr.at[7], sdx.at[7], rdx.at[7])
    for sub in range(4):
        rows = pl.ds(128 * sub, 128)
        deliver(2, sub, dall[7, core, rows, :] + dxr[7, rows, :].astype(F32))
    for j in range(4):
        got(rrecv.at[pl.ds(32 * j, 32)], so.at[j], ro.at[j])
    res_ref[...] = rrecv[...].astype(F32).T.astype(BF)
    ring_step(3)
    for sub in range(4):
        cols = pl.ds(128 * sub, 128)
        for n in (2, 0, 1):
            for j in range(4):
                got(fr.at[n, sub, pl.ds(32 * j, 32)], sf.at[n, sub, j], rf.at[n, sub, j])
        total = fr[0, sub].astype(F32) + fr[1, sub].astype(F32) + fr[2, sub].astype(F32)
        new_ref[:, cols] = par_ref[:, cols] + total * (0.5 / math.sqrt(24576))

    for wait in sent:
        wait()

    @pl.loop(0, 8)
    def _(pos):
        send(dxs.at[pos], dxr.at[pos], sdx.at[pos], rdx.at[pos], partner).wait_send()
    for way in range(2):
        for sub in range(4):
            for j in range(4):
                send(*delivery(way, sub, j)).wait_send()
    for step in range(3):
        for n, (way, subs) in enumerate(ways):
            if step or n < 2:
                for sub in subs:
                    send(gs.at[way, step, sub], gr.at[way, step, sub], sg.at[way, step, sub], rg.at[way, step, sub],
                         along(1 if way == 0 else -1)).wait_send()


def on_device(records, measured, markov_params, seg_lengths):
    dma = pltpu.SemaphoreType.DMA
    new, res = pl.pallas_call(
        body,
        out_shape=(jax.ShapeDtypeStruct((128, 512), F32), jax.ShapeDtypeStruct((384, 128), BF)),
        in_specs=[pl.BlockSpec(memory_space=pltpu.SMEM)] + [pl.BlockSpec(memory_space=pltpu.HBM)] * 3,
        out_specs=(pl.BlockSpec(memory_space=pltpu.VMEM), pl.BlockSpec(memory_space=pltpu.VMEM)),
        scratch_shapes=[
            pltpu.VMEM((384, 128), BF),
            pltpu.VMEM((128, 512), F32),
            dma((2,)),
            pltpu.VMEM((128, 512), BF),
            pltpu.VMEM((2048, 512), BF),
            pltpu.VMEM((4, HALO + SPAN, 128), BF),
            pltpu.VMEM((512, HALO + SPAN), BF),
            pltpu.VMEM((128, 384), BF),
            pltpu.VMEM((4, 32, 384), BF),
            pltpu.VMEM((128, SPAN), F32),
            pltpu.VMEM((SPAN, 128), F32),
            pltpu.VMEM((8, 128), F32),
            pltpu.VMEM((4, 8, 128), F32),
            pltpu.VMEM((1664, 256), F32),
            pltpu.VMEM((1552, 128), F32),
            pltpu.VMEM((1544, 128), F32),
            pltpu.VMEM((1744, 128), F32),
            pltpu.VMEM((1736, 128), F32),
            pltpu.VMEM((1732, 128), F32),
            pltpu.VMEM((2, 1712, 256), BF),
            pltpu.VMEM((4, 32, 384), BF),
            pltpu.VMEM((128, 384), BF),
            pltpu.VMEM((8, 2, 512, 128), F32),
            pltpu.VMEM((8, 512, 128), BF),
            pltpu.VMEM((8, 512, 128), BF),
            pltpu.VMEM((2, 3, 4, 128, 128), BF),
            pltpu.VMEM((2, 3, 4, 128, 128), BF),
            pltpu.VMEM((3, 4, 128, 128), BF),
            pltpu.VMEM((3, 4, 128, 128), BF),
            dma((4,)), dma((4,)), dma((4,)), dma((4, 3)), dma((2, 3)), dma((16,)), dma((4,)), dma((4,)), dma((4,)), dma((4,)),
            dma((4,)), dma((4,)), dma((1,)), dma((1,)),
            dma((2, 4, 4)), dma((2, 4, 4)), dma((8, 4)), dma((8, 4)),
            dma((8,)), dma((8,)), dma((2, 3, 4)), dma((2, 3, 4)), dma((3, 4, 4)), dma((3, 4, 4)),
        ],
        compiler_params=pltpu.CompilerParams(collective_id=0, has_side_effects=True, vmem_limit_bytes=34 * 1024 * 1024),
        name="gradient_step",
    )(seg_lengths, *(pltpu.with_memory_space_constraint(a, pltpu.HBM) for a in (records, measured, markov_params.reshape(128, 512))))
    return new.reshape(1, 128, 512), res


def solution(mesh):
    in_specs = (P("tm", "grp"), P("tm", "grp"), P("tm", "grp", None), P("tm"))
    out_specs = (P("tm", "grp", None), P("tm", "grp"))
    return jax.shard_map(on_device, mesh=mesh, in_specs=in_specs, out_specs=out_specs, check_vma=False)
```
